32 devices in a mesh: grp: 2 (over x), wide: 16 (over z, y, core).
Axes of the slice: x: 2, y: 2, z: 4, core: 2. Of those that a mesh axis runs over, the one named last changes fastest.
Arguments:
- hidden_in: bfloat16 [128, 4096], P(('grp', 'wide')), parts along dimension 0, may hold values from -6 to 6
- ffn_gain: float32 [4096], replicated, may hold values from 0.1 to 1.9
- gate_weight: bfloat16 [4096, 14336], P(None, 'wide'), may hold values from -0.09375 to 0.09375
- up_weight: bfloat16 [4096, 14336], P(None, 'wide'), may hold values from -0.09375 to 0.09375
- down_weight: bfloat16 [14336, 4096], P('wide'), may hold values from -0.046875 to 0.046875
- final_gain: float32 [4096], replicated, may hold values from 0.1 to 1.9
- codes: bfloat16 [256, 128, 4096], P(('grp', 'wide')), parts along dimension 0, may hold values from -1 to 1
- scales: float32 [256, 128, 32], P(('grp', 'wide')), parts along dimension 0, may hold values from 0.5 to 5
- counts: int32 [256], P('grp'), parts along dimension 0, may hold values from 1 to 128, 10240 in all
- list_slot: int32 [256], P('grp'), parts along dimension 0, may hold values from 0 to 127, as said below
- probes: int32 [128, 8], P(('grp', 'wide')), parts along dimension 0, may hold values from 0 to 127, as said below
Outputs:
- top_scores: float32 [128, 8], P(('grp', 'wide')), parts along dimension 0
The draws below stay inside these ranges and needn't reach their ends.
There are 2 independent parts, one for each index of `grp`. The reference program is written for one: setup_inputs(seed, part) draws one part's arguments, and reference() takes and returns one part's arrays. A program takes and returns all parts, laid end to end along the dimension named above; an argument that names none is the same for every part. Nothing has to cross between parts.
Inputs may be any that keep to these rules, and one draw needn't show every extreme that they name: Each query names 8 different lists. List l is held by device list_slot[l] // 8; of the 32 probes of one device's queries at most 2 name lists held by one device, and some devices are named 2 times by the queries of every device. `list_slot`: each storage row holds exactly one list. The valid rows of a list are its first counts[l] rows; some list is full.
All inputs are finite; a program needn't handle non-finite values.
Results may differ from the reference program's by a relative error of at most 0.002.
Values may be sent and summed in bfloat16 or wider, within the bound.
No kernel may reach another device: no remote copies, remote signals or barrier semaphores. Data moves between devices by JAX's collectives and lax.ppermute only.
A program may use at most 128 MiB of HBM per device.

```python
import math
import jax
import jax.numpy as jnp
import numpy as np
from jax import lax

D = 4096
FF = 14336
Q_DEV = 4
LISTS_DEV = 8
LIST_ROWS = 128
PROBES = 8
K_TOP = 8
QUERIES = 64
NLISTS = 128
CAP = 2
ROWS_HELD = 10240


def layout(key):
    slot_to_list = jax.random.permutation(jax.random.fold_in(key, 101), NLISTS).astype(jnp.int32)
    list_slot = jnp.zeros((NLISTS,), jnp.int32).at[slot_to_list].set(jnp.arange(NLISTS, dtype=jnp.int32))
    return (slot_to_list, list_slot)


def draw_list_slot(key, part):
    return layout(key)[1]


def draw_probes(key, part):
    slot_to_list = layout(key)[0]
    devices = QUERIES // Q_DEV
    pair_total = PROBES * Q_DEV
    choices_total = devices * CAP
    candidate = jnp.arange(choices_total, dtype=jnp.int32)
    cand_owner = candidate // CAP
    hot_order = jax.random.permutation(jax.random.fold_in(key, 102), devices)
    hot_flag = jnp.zeros((devices,), jnp.int32).at[hot_order[:4]].set(1)
    noise = jax.random.randint(jax.random.fold_in(key, 103), (devices, choices_total), 0, 65536)
    ranked = noise * choices_total + candidate[None, :] + hot_flag[cand_owner][None, :] * (1 << 26)
    picked = lax.top_k(ranked, pair_total)[1].astype(jnp.int32)
    order_noise = jax.random.randint(jax.random.fold_in(key, 104), (devices, pair_total), 0, 65536)
    order_key = order_noise * pair_total + jnp.arange(pair_total, dtype=jnp.int32)[None, :]
    order = jnp.argsort(order_key, axis=1, stable=True)
    picked = jnp.take_along_axis(picked, order, axis=1)
    base = jax.random.randint(jax.random.fold_in(key, 105), (devices, devices), 0, LISTS_DEV)
    owner = picked // CAP
    copy_index = picked % CAP
    local = (jnp.take_along_axis(base, owner, axis=1) + copy_index) % LISTS_DEV
    slot = owner * LISTS_DEV + local
    return slot_to_list[slot].reshape(QUERIES, PROBES).astype(jnp.int32)


def levels(key, extent, cuts, low, high):
    loudness, own = 1.0, jax.random.fold_in(key, 6)
    for dim, shards_of in cuts:
        draws = jnp.exp(jax.random.uniform(jax.random.fold_in(own, dim), (shards_of,), jnp.float32, low / len(cuts), high / len(cuts)))
        loudness = loudness * jnp.repeat(draws, extent[dim] // shards_of).reshape([-1 if axis == dim else 1 for axis in range(len(extent))])
    return loudness


def profile(amount, total, most, skew):
    loads = [(1 << 20) // math.isqrt(grade ** skew) + 1 for grade in range(2, amount + 1)]
    rest, given = total - most - (amount - 1), [1] * (amount - 1)
    while rest > 0:
        movable = [i for i in range(amount - 1) if given[i] < most]
        whole, left = sum([loads[i] for i in movable]), rest
        for i in movable:
            extra = min(most - given[i], max(1, left * loads[i] // whole), rest)
            given[i] = given[i] + extra
            rest = rest - extra
    return np.array([most] + given)


def uneven_parts(stream_key, count, total, limit, skew):
    if count == 2:
        one = jax.random.randint(stream_key, (), max(1, total - limit), min(limit, total - 1) + 1)
        return jnp.stack([one, total - one])
    tallies = jnp.asarray(profile(count, total, limit, skew), jnp.int32)
    pairs = (count - 1) // 2
    giver, sink = tallies[1:1 + 2 * pairs:2], tallies[2:2 + 2 * pairs:2]
    margin = jnp.minimum(giver - 1, limit - sink)
    shifted = jax.random.randint(jax.random.fold_in(stream_key, 1), (pairs,), 0, 1 << 20) % (margin + 1)
    tallies = tallies.at[1:1 + 2 * pairs:2].set(giver - shifted).at[2:2 + 2 * pairs:2].set(sink + shifted)
    return tallies[jax.random.permutation(jax.random.fold_in(stream_key, 2), count)]


def scatter_about(rng, dims, spread, bound, pieces=(), held_as=jnp.bfloat16):
    drawn = spread * jax.random.normal(rng, dims, jnp.float32)
    if pieces:
        drawn = drawn * levels(rng, dims, pieces, -0.22, 0.18)
    return jnp.clip(drawn, -bound, bound).astype(held_as)


def setup_inputs(seed: int = 0, part: int = 0) -> dict:
    streams_of = jax.random.split(jax.random.key(seed), 12)
    own_keys = jax.random.split(jax.random.fold_in(streams_of[11], part), 12)
    return {
        "hidden_in": scatter_about(own_keys[0], (QUERIES, D), 1.0, 6.0, ((0, 16),)),
        "ffn_gain": jnp.clip(1.0 + 0.18 * jax.random.normal(streams_of[1], (D,), jnp.float32), 0.1, 1.9),
        "gate_weight": scatter_about(streams_of[2], (D, FF), D ** -0.5, 0.09375, ((1, 16),)),
        "up_weight": scatter_about(streams_of[3], (D, FF), D ** -0.5, 0.09375, ((1, 16),)),
        "down_weight": scatter_about(streams_of[4], (FF, D), FF ** -0.5, 0.046875, ((0, 16),)),
        "final_gain": jnp.clip(1.0 + 0.18 * jax.random.normal(streams_of[5], (D,), jnp.float32), 0.1, 1.9),
        "codes": jnp.clip(jax.random.uniform(own_keys[6], (NLISTS, LIST_ROWS, D), jnp.float32, -1.0, 1.0) * levels(own_keys[6], (NLISTS, LIST_ROWS, D), ((0, 16),), -0.4, 0.0), -1.0, 1.0).astype(jnp.bfloat16),
        "scales": jnp.clip(jnp.exp(math.log(5.0) - 2.3025851 * jax.random.uniform(own_keys[7], (NLISTS, LIST_ROWS, D // 128), jnp.float32) ** levels(own_keys[7], (NLISTS, LIST_ROWS, D // 128), ((0, 16),), -0.2, 0.2)), 0.5, 5.0),
        "counts": uneven_parts(own_keys[8], NLISTS, ROWS_HELD, LIST_ROWS, 2).astype(jnp.int32),
        "list_slot": draw_list_slot(jax.random.fold_in(jax.random.fold_in(streams_of[11], part), 71), part),
        "probes": draw_probes(jax.random.fold_in(jax.random.fold_in(streams_of[11], part), 71), part),
    }


floor_score = -1e+30

def reference(hidden_in, ffn_gain, gate_weight, up_weight, down_weight, final_gain, codes, scales, counts, list_slot, probes):
    rows = hidden_in.astype(jnp.float32)
    normed = (rows * lax.rsqrt(lax.optimization_barrier(jnp.mean(rows * rows, axis=-1, keepdims=True)) + 1e-05) * ffn_gain).astype(jnp.bfloat16)
    gate = jnp.dot(normed, gate_weight, preferred_element_type=jnp.float32)
    upward = jnp.dot(normed, up_weight, preferred_element_type=jnp.float32)
    activated = (jax.nn.silu(gate) * upward).astype(jnp.bfloat16)
    ffn_out = jnp.dot(activated, down_weight, preferred_element_type=jnp.float32)
    scaled = final_gain * (rows + ffn_out)
    embedded = (scaled * lax.rsqrt(lax.optimization_barrier(jnp.sum(scaled * scaled, axis=-1, keepdims=True)) + 1e-06)).astype(jnp.bfloat16)
    blocks = D // 128

    def one_query(item):
        vector, listed = item
        slot_ids = list_slot[listed].astype(jnp.int32)
        stored = codes[slot_ids].astype(jnp.float32).reshape(PROBES, LIST_ROWS, blocks, 128)
        partial_sums = jnp.einsum('jrbk,bk->jrb', stored, vector.astype(jnp.float32).reshape(blocks, 128))
        total = lax.optimization_barrier(jnp.sum(partial_sums * scales[slot_ids], axis=-1))
        alive = jnp.arange(LIST_ROWS, dtype=jnp.int32)[None, :] < counts[listed][:, None]
        masked = jnp.where(alive, total, floor_score)
        return lax.top_k(masked.reshape(-1), K_TOP)[0]
    return lax.map(one_query, (embedded, probes))
```

```python
import functools

import jax
import jax.numpy as jnp
from jax import lax
from jax.experimental import pallas as pl
from jax.experimental.pallas import tpu as pltpu
from jax.sharding import PartitionSpec as P

PROBES = 8
K_TOP = 8
BLOCK = 128
LANES = 128

floor_score = -1e30

VMEM = pltpu.VMEM


def call(kernel, out_shape, args, vmem, cost=None, scratch=()):
    many = isinstance(out_shape, (list, tuple))
    return pl.pallas_call(
        kernel,
        out_shape=out_shape,
        in_specs=[pl.BlockSpec(memory_space=VMEM)] * len(args),
        out_specs=[pl.BlockSpec(memory_space=VMEM)] * len(out_shape)
        if many
        else pl.BlockSpec(memory_space=VMEM),
        scratch_shapes=list(scratch),
        compiler_params=pltpu.CompilerParams(vmem_limit_bytes=vmem),
        cost_estimate=cost,
    )(*args)


def shaped(shape, dtype):
    return jax.ShapeDtypeStruct(shape, dtype)


def norm_kernel(hidden_ref, gain_ref, out_ref):
    rows = hidden_ref[...].astype(jnp.float32)
    scale = lax.rsqrt(jnp.mean(rows * rows, axis=-1, keepdims=True) + 1e-05)
    normed = (rows * scale * gain_ref[...]).astype(jnp.bfloat16)
    for k in range(out_ref.shape[0]):
        out_ref[k] = normed


def route_kernel(lists_dev, capacity, probes_ref, slot_ref, count_ref, out_ref):
    q_dev, probes = probes_ref.shape
    lists = slot_ref.shape[1]
    pairs = q_dev * probes
    slots = out_ref.shape[0]
    ids = jnp.concatenate(
        [jnp.broadcast_to(probes_ref[q : q + 1, :], (probes, probes)) for q in range(q_dev)], axis=0
    )
    sub = lax.broadcasted_iota(jnp.int32, (pairs, probes), 0)
    lane = lax.broadcasted_iota(jnp.int32, (pairs, probes), 1)
    ids = jnp.sum(jnp.where(sub % probes == lane, ids, 0), axis=1, keepdims=True)
    hit = lax.broadcasted_iota(jnp.int32, (pairs, lists), 1) == ids
    slot = jnp.sum(jnp.where(hit, slot_ref[...], 0), axis=1, keepdims=True)
    valid = jnp.sum(jnp.where(hit, count_ref[...], 0), axis=1, keepdims=True)
    owner = slot // lists_dev
    local = slot % lists_dev
    p_sub = lax.broadcasted_iota(jnp.int32, (pairs, pairs), 0)
    p_lane = lax.broadcasted_iota(jnp.int32, (pairs, pairs), 1)
    diagonal = p_sub == p_lane

    def as_row(column):
        return jnp.sum(jnp.where(diagonal, column, 0), axis=0, keepdims=True)

    owner_row = as_row(owner)
    rank_row = jnp.sum(
        jnp.where((owner == owner_row) & (p_sub < p_lane), 1, 0), axis=0, keepdims=True
    )
    target_row = owner_row * capacity + rank_row
    here = lax.broadcasted_iota(jnp.int32, (slots, pairs), 0) == target_row
    pair_row = lax.broadcasted_iota(jnp.int32, (slots, pairs), 1)

    def of_slot(row):
        return jnp.sum(jnp.where(here, row, 0), axis=1, keepdims=True)

    query = of_slot(pair_row // probes + 1) - 1
    place = lax.broadcasted_iota(jnp.int32, (slots, LANES), 1)
    out = jnp.where(place == 0, query, 0)
    out = jnp.where(place == 1, of_slot(as_row(local)), out)
    out_ref[...] = jnp.where(place == 2, of_slot(as_row(valid)), out)


def ffn_kernel(
    k_chunk, n_chunk, same_ref, other_ref, gate_ref, up_ref, down_ref, own_ref, send_ref,
    rows_ref, gate_acc, up_acc, act_ref,
):
    chips, q_dev, width = same_ref.shape
    half = chips * q_dev
    rows_ref[:half, :] = same_ref[...].reshape(half, width)
    rows_ref[half:, :] = other_ref[...].reshape(half, width)
    gate_acc[...] = jnp.zeros_like(gate_acc)
    up_acc[...] = jnp.zeros_like(up_acc)

    @pl.loop(0, width // k_chunk)
    def _(step):
        span = pl.ds(pl.multiple_of(step * k_chunk, k_chunk), k_chunk)
        x = rows_ref[:, span]
        gate_acc[...] += jnp.dot(x, gate_ref[span, :], preferred_element_type=jnp.float32)
        up_acc[...] += jnp.dot(x, up_ref[span, :], preferred_element_type=jnp.float32)

    gate = gate_acc[...]
    act_ref[...] = (gate / (1.0 + jnp.exp(-gate)) * up_acc[...]).astype(jnp.bfloat16)

    @pl.loop(0, width // n_chunk)
    def _(step):
        span = pl.ds(pl.multiple_of(step * n_chunk, n_chunk), n_chunk)
        out = jnp.dot(act_ref[...], down_ref[:, span], preferred_element_type=jnp.float32)
        own_ref[:, span] = out[:half]
        send_ref[:, span] = out[half:].astype(jnp.bfloat16)


def add_kernel(own_ref, came_ref, out_ref):
    total = own_ref[...] + came_ref[...].astype(jnp.float32)
    out_ref[...] = total.astype(jnp.bfloat16).reshape(out_ref.shape)


def embed_kernel(parts_ref, hidden_ref, gain_ref, route_ref, out_ref):
    chips, q_dev, width = parts_ref.shape
    total = parts_ref[0].astype(jnp.float32)
    for k in range(1, chips):
        total += parts_ref[k].astype(jnp.float32)
    scaled = gain_ref[...] * (hidden_ref[...].astype(jnp.float32) + total)
    embedded = scaled * lax.rsqrt(jnp.sum(scaled * scaled, axis=-1, keepdims=True) + 1e-06)
    query = route_ref[:, 0:1]
    sent = jnp.zeros((query.shape[0], width), jnp.float32)
    for q in range(q_dev):
        sent = jnp.where(query == q, embedded[q : q + 1, :], sent)
    out_ref[:, :, :width] = sent.astype(jnp.bfloat16).reshape(out_ref.shape[:2] + (width,))
    lane = lax.broadcasted_iota(jnp.int32, (query.shape[0], LANES), 1)
    local = jnp.where(lane == 0, route_ref[:, 1:2], 0).astype(jnp.float32)
    out_ref[:, :, width:] = local.astype(jnp.bfloat16).reshape(out_ref.shape[:2] + (LANES,))


def score_kernel(came_ref, codes_ref, scales_ref, out_ref, rows_ref):
    sources, slots, _ = came_ref.shape
    lists, list_rows, width = codes_ref.shape
    pairs = sources * slots
    rows_ref[...] = came_ref[...].reshape(rows_ref.shape)
    local = rows_ref[:, width : width + 1].astype(jnp.float32).astype(jnp.int32)

    def one_list(index, picked):
        scale = scales_ref[index]
        total = jnp.zeros((pairs, list_rows), jnp.float32)
        for block in range(width // BLOCK):
            span = slice(block * BLOCK, (block + 1) * BLOCK)
            part = lax.dot_general(
                rows_ref[:, span],
                codes_ref[index, :, span],
                (((1,), (1,)), ((), ())),
                preferred_element_type=jnp.float32,
            )
            total += part * scale[block : block + 1, :]
        return jnp.where(local == index, total, picked)

    picked = lax.fori_loop(0, lists, one_list, jnp.zeros((pairs, list_rows), jnp.float32))
    out_ref[...] = picked.reshape(out_ref.shape)


def best_kernel(back_ref, route_ref, out_ref):
    q_dev, count = out_ref.shape
    sources, slots, list_rows = back_ref.shape
    pairs = sources * slots
    scores = back_ref[...].reshape(pairs, list_rows)
    query = route_ref[:, 0:1]
    row = lax.broadcasted_iota(jnp.int32, (pairs, list_rows), 1)
    place = lax.broadcasted_iota(jnp.int32, (pairs, list_rows), 0) * list_rows + row
    alive = row < route_ref[:, 2:3]
    column = lax.broadcasted_iota(jnp.int32, (1, count), 1)
    for q in range(q_dev):
        left = jnp.where(alive & (query == q), scores, floor_score)
        best = jnp.zeros((1, count), jnp.float32)
        for rank in range(count):
            top = jnp.max(left, axis=(0, 1), keepdims=True)
            best = jnp.where(column == rank, top, best)
            if rank + 1 < count:
                first = jnp.min(
                    jnp.where(left == top, place, pairs * list_rows), axis=(0, 1), keepdims=True
                )
                left = jnp.where(place == first, floor_score * 2, left)
        out_ref[q : q + 1, :] = best


def body(
    hidden_in,
    ffn_gain,
    gate_weight,
    up_weight,
    down_weight,
    final_gain,
    codes,
    scales,
    counts,
    list_slot,
    probes,
):
    q_dev, width = hidden_in.shape
    hidden_units = gate_weight.shape[1]
    n = lax.axis_size("wide")
    chips = n // 2
    half = chips * q_dev
    rows = 2 * half
    lists_dev, list_rows, _ = codes.shape
    capacity = (q_dev * PROBES + n - 1) // n
    groups = [[core + 2 * k for k in range(chips)] for core in range(2)]
    swap = [(i, i ^ 1) for i in range(n)]
    mib = 1 << 20
    f32, bf16 = jnp.float32, jnp.bfloat16

    def exchange(x, axis_index_groups=None):
        return lax.all_to_all(
            x, "wide", 0, 0, axis_index_groups=axis_index_groups, tiled=True
        )

    gate_near = pltpu.with_memory_space_constraint(gate_weight, VMEM)
    up_near = pltpu.with_memory_space_constraint(up_weight, VMEM)
    down_near = pltpu.with_memory_space_constraint(down_weight, VMEM)
    codes_near = pltpu.with_memory_space_constraint(codes, VMEM)

    normed = call(
        norm_kernel, shaped((chips, q_dev, width), bf16), (hidden_in, ffn_gain[None]), 8 * mib
    )
    route = call(
        functools.partial(route_kernel, lists_dev, capacity),
        shaped((n * capacity, LANES), jnp.int32),
        (probes, list_slot[None], counts[None]),
        8 * mib,
    )
    same = exchange(normed, groups)
    other = lax.ppermute(same, "wide", swap)
    own, sent = call(
        functools.partial(ffn_kernel, 512, 512),
        [shaped((half, width), f32), shaped((half, width), bf16)],
        (same, other, gate_near, up_near, down_near),
        20 * mib,
        scratch=[
            VMEM((rows, width), bf16),
            VMEM((rows, hidden_units), f32),
            VMEM((rows, hidden_units), f32),
            VMEM((rows, hidden_units), bf16),
        ],
    )
    came = lax.ppermute(sent, "wide", swap)
    pairs_sum = call(add_kernel, shaped((chips, q_dev, width), bf16), (own, came), 16 * mib)
    parts = exchange(pairs_sum, groups)
    queries = call(
        embed_kernel,
        shaped((n, capacity, width + LANES), bf16),
        (parts, hidden_in, final_gain[None], route),
        16 * mib,
    )
    recv = exchange(queries)
    scores = call(
        score_kernel,
        shaped((n, capacity, list_rows), f32),
        (recv, codes_near, jnp.swapaxes(scales, 1, 2)),
        20 * mib,
        scratch=[VMEM((n * capacity, width + LANES), bf16)],
    )
    back = exchange(scores)
    return call(best_kernel, shaped((q_dev, K_TOP), f32), (back, route), 8 * mib)


def solution(mesh):
    in_specs = (
        P(("grp", "wide"), None),
        P(),
        P(None, "wide"),
        P(None, "wide"),
        P("wide", None),
        P(),
        P(("grp", "wide"), None, None),
        P(("grp", "wide"), None, None),
        P("grp"),
        P("grp"),
        P(("grp", "wide"), None),
    )
    out_specs = P(("grp", "wide"), None)
    return jax.shard_map(body, mesh=mesh, in_specs=in_specs, out_specs=out_specs, check_vma=False)
```

```python
import functools

import jax
import jax.numpy as jnp
from jax import lax
from jax.experimental import pallas as pl
from jax.experimental.pallas import tpu as pltpu
from jax.sharding import PartitionSpec as P

PROBES = 8
K_TOP = 8
BLOCK = 128
LANES = 128

floor_score = -1e30

VMEM = pltpu.VMEM


def call(kernel, out_shape, args, vmem, cost=None, scratch=()):
    many = isinstance(out_shape, (list, tuple))
    return pl.pallas_call(
        kernel,
        out_shape=out_shape,
        in_specs=[pl.BlockSpec(memory_space=VMEM)] * len(args),
        out_specs=[pl.BlockSpec(memory_space=VMEM)] * len(out_shape)
        if many
        else pl.BlockSpec(memory_space=VMEM),
        scratch_shapes=list(scratch),
        compiler_params=pltpu.CompilerParams(vmem_limit_bytes=vmem),
        cost_estimate=cost,
    )(*args)


def ahead(*arrays):
    total = sum(a.size * a.dtype.itemsize for a in arrays)
    return pl.CostEstimate(flops=1000 * total, bytes_accessed=1 << 20, transcendentals=0)


def shaped(shape, dtype):
    return jax.ShapeDtypeStruct(shape, dtype)


def norm_kernel(hidden_ref, gain_ref, out_ref):
    rows = hidden_ref[...].astype(jnp.float32)
    scale = lax.rsqrt(jnp.mean(rows * rows, axis=-1, keepdims=True) + 1e-05)
    normed = (rows * scale * gain_ref[...]).astype(jnp.bfloat16)
    for k in range(out_ref.shape[0]):
        out_ref[k] = normed


def route_kernel(lists_dev, capacity, probes_ref, slot_ref, count_ref, after_ref, out_ref):
    q_dev, probes = probes_ref.shape
    lists = slot_ref.shape[1]
    pairs = q_dev * probes
    slots = out_ref.shape[0]
    ids = jnp.concatenate(
        [jnp.broadcast_to(probes_ref[q : q + 1, :], (probes, probes)) for q in range(q_dev)], axis=0
    )
    sub = lax.broadcasted_iota(jnp.int32, (pairs, probes), 0)
    lane = lax.broadcasted_iota(jnp.int32, (pairs, probes), 1)
    ids = jnp.sum(jnp.where(sub % probes == lane, ids, 0), axis=1, keepdims=True)
    hit = lax.broadcasted_iota(jnp.int32, (pairs, lists), 1) == ids
    slot = jnp.sum(jnp.where(hit, slot_ref[...], 0), axis=1, keepdims=True)
    valid = jnp.sum(jnp.where(hit, count_ref[...], 0), axis=1, keepdims=True)
    owner = slot // lists_dev
    local = slot % lists_dev
    p_sub = lax.broadcasted_iota(jnp.int32, (pairs, pairs), 0)
    p_lane = lax.broadcasted_iota(jnp.int32, (pairs, pairs), 1)
    diagonal = p_sub == p_lane

    def as_row(column):
        return jnp.sum(jnp.where(diagonal, column, 0), axis=0, keepdims=True)

    owner_row = as_row(owner)
    rank_row = jnp.sum(
        jnp.where((owner == owner_row) & (p_sub < p_lane), 1, 0), axis=0, keepdims=True
    )
    target_row = owner_row * capacity + rank_row
    here = lax.broadcasted_iota(jnp.int32, (slots, pairs), 0) == target_row
    pair_row = lax.broadcasted_iota(jnp.int32, (slots, pairs), 1)

    def of_slot(row):
        return jnp.sum(jnp.where(here, row, 0), axis=1, keepdims=True)

    query = of_slot(pair_row // probes + 1) - 1
    place = lax.broadcasted_iota(jnp.int32, (slots, LANES), 1)
    out = jnp.where(place == 0, query, 0)
    out = jnp.where(place == 1, of_slot(as_row(local)), out)
    out_ref[...] = jnp.where(place == 2, of_slot(as_row(valid)), out)


def ffn_kernel(
    k_chunk, n_chunk, same_ref, other_ref, gate_ref, up_ref, down_ref, after_ref, own_ref, send_ref,
    rows_ref, gate_acc, up_acc, act_ref,
):
    chips, q_dev, width = same_ref.shape
    half = chips * q_dev
    rows_ref[:half, :] = same_ref[...].reshape(half, width)
    rows_ref[half:, :] = other_ref[...].reshape(half, width)
    gate_acc[...] = jnp.zeros_like(gate_acc)
    up_acc[...] = jnp.zeros_like(up_acc)

    @pl.loop(0, width // k_chunk)
    def _(step):
        span = pl.ds(pl.multiple_of(step * k_chunk, k_chunk), k_chunk)
        x = rows_ref[:, span]
        gate_acc[...] += jnp.dot(x, gate_ref[span, :], preferred_element_type=jnp.float32)
        up_acc[...] += jnp.dot(x, up_ref[span, :], preferred_element_type=jnp.float32)

    gate = gate_acc[...]
    act_ref[...] = (gate / (1.0 + jnp.exp(-gate)) * up_acc[...]).astype(jnp.bfloat16)

    @pl.loop(0, width // n_chunk)
    def _(step):
        span = pl.ds(pl.multiple_of(step * n_chunk, n_chunk), n_chunk)
        out = jnp.dot(act_ref[...], down_ref[:, span], preferred_element_type=jnp.float32)
        own_ref[:, span] = out[:half]
        send_ref[:, span] = out[half:].astype(jnp.bfloat16)


def add_kernel(own_ref, came_ref, out_ref):
    total = own_ref[...] + came_ref[...].astype(jnp.float32)
    out_ref[...] = total.astype(jnp.bfloat16).reshape(out_ref.shape)


def embed_kernel(parts_ref, hidden_ref, gain_ref, route_ref, out_ref):
    chips, q_dev, width = parts_ref.shape
    total = parts_ref[0].astype(jnp.float32)
    for k in range(1, chips):
        total += parts_ref[k].astype(jnp.float32)
    scaled = gain_ref[...] * (hidden_ref[...].astype(jnp.float32) + total)
    embedded = scaled * lax.rsqrt(jnp.sum(scaled * scaled, axis=-1, keepdims=True) + 1e-06)
    query = route_ref[:, 0:1]
    sent = jnp.zeros((query.shape[0], width), jnp.float32)
    for q in range(q_dev):
        sent = jnp.where(query == q, embedded[q : q + 1, :], sent)
    out_ref[:, :, :width] = sent.astype(jnp.bfloat16).reshape(out_ref.shape[:2] + (width,))
    lane = lax.broadcasted_iota(jnp.int32, (query.shape[0], LANES), 1)
    local = jnp.where(lane == 0, route_ref[:, 1:2], 0).astype(jnp.float32)
    out_ref[:, :, width:] = local.astype(jnp.bfloat16).reshape(out_ref.shape[:2] + (LANES,))


def score_kernel(came_ref, codes_ref, scales_ref, out_ref, rows_ref):
    sources, slots, _ = came_ref.shape
    lists, list_rows, width = codes_ref.shape
    pairs = sources * slots
    came = came_ref[...].reshape(pairs, width + LANES)
    nothing = jnp.zeros((pairs, BLOCK), jnp.bfloat16)
    for block in range(width // BLOCK):
        span = slice(block * BLOCK, (block + 1) * BLOCK)
        kept = block % 2
        rows_ref[kept * pairs : (kept + 1) * pairs, span] = came[:, span]
        rows_ref[(1 - kept) * pairs : (2 - kept) * pairs, span] = nothing
    local = came[:, width : width + 1].astype(jnp.float32).astype(jnp.int32)

    def two_lists(index, picked):
        first = index * 2
        scale = jnp.concatenate([scales_ref[first], scales_ref[first + 1]], axis=1)
        total = jnp.zeros((pairs, 2 * list_rows), jnp.float32)
        for step in range(width // (2 * BLOCK)):
            span = slice(step * 2 * BLOCK, (step + 1) * 2 * BLOCK)
            part = lax.dot_general(
                rows_ref[:, span],
                codes_ref[pl.ds(first, 2), :, span].reshape(2 * list_rows, 2 * BLOCK),
                (((1,), (1,)), ((), ())),
                preferred_element_type=jnp.float32,
            )
            total += part[:pairs] * scale[2 * step : 2 * step + 1, :]
            total += part[pairs:] * scale[2 * step + 1 : 2 * step + 2, :]
        picked = jnp.where(local == first, total[:, :list_rows], picked)
        return jnp.where(local == first + 1, total[:, list_rows:], picked)

    picked = lax.fori_loop(0, lists // 2, two_lists, jnp.zeros((pairs, list_rows), jnp.float32))
    out_ref[...] = picked.reshape(out_ref.shape)


def best_kernel(back_ref, route_ref, out_ref):
    q_dev, count = out_ref.shape
    sources, slots, list_rows = back_ref.shape
    pairs = sources * slots
    scores = back_ref[...].reshape(pairs, list_rows)
    query = route_ref[:, 0:1]
    alive = lax.broadcasted_iota(jnp.int32, (pairs, list_rows), 1) < route_ref[:, 2:3]
    left = jnp.concatenate(
        [jnp.where(alive & (query == q), scores, floor_score)[None] for q in range(q_dev)], axis=0
    )
    column = lax.broadcasted_iota(jnp.int32, (q_dev, count), 1)
    best = jnp.zeros((q_dev, count), jnp.float32)
    filled = jnp.zeros((q_dev, 1), jnp.float32)
    for rank in range(count):
        top = jnp.max(jnp.max(left, axis=1), axis=-1, keepdims=True)
        best = jnp.where(column >= filled.astype(jnp.int32), top, best)
        if rank + 1 < count:
            same = left == top[:, :, None]
            filled += jnp.sum(
                jnp.sum(jnp.where(same, 1.0, 0.0), axis=1), axis=-1, keepdims=True
            )
            left = jnp.where(same, floor_score * 2, left)
    out_ref[...] = best


def body(
    hidden_in,
    ffn_gain,
    gate_weight,
    up_weight,
    down_weight,
    final_gain,
    codes,
    scales,
    counts,
    list_slot,
    probes,
):
    q_dev, width = hidden_in.shape
    hidden_units = gate_weight.shape[1]
    n = lax.axis_size("wide")
    chips = n // 2
    half = chips * q_dev
    rows = 2 * half
    lists_dev, list_rows, _ = codes.shape
    capacity = (q_dev * PROBES + n - 1) // n
    groups = [[core + 2 * k for k in range(chips)] for core in range(2)]
    swap = [(i, i ^ 1) for i in range(n)]
    mib = 1 << 20
    f32, bf16 = jnp.float32, jnp.bfloat16

    def exchange(x, axis_index_groups=None):
        return lax.all_to_all(
            x, "wide", 0, 0, axis_index_groups=axis_index_groups, tiled=True
        )

    gate_near = pltpu.with_memory_space_constraint(gate_weight, VMEM)
    up_near = pltpu.with_memory_space_constraint(up_weight, VMEM)
    down_near = pltpu.with_memory_space_constraint(down_weight, VMEM)
    codes_near = pltpu.with_memory_space_constraint(codes, VMEM)

    normed = call(
        norm_kernel, shaped((chips, q_dev, width), bf16), (hidden_in, ffn_gain[None]), 8 * mib,
        cost=ahead(gate_weight, up_weight, down_weight),
    )
    same = exchange(normed, groups)
    other = lax.ppermute(same, "wide", swap)
    route = call(
        functools.partial(route_kernel, lists_dev, capacity),
        shaped((n * capacity, LANES), jnp.int32),
        (probes, list_slot[None], counts[None], same),
        8 * mib,
    )
    own, sent = call(
        functools.partial(ffn_kernel, 512, 512),
        [shaped((half, width), f32), shaped((half, width), bf16)],
        (same, other, gate_near, up_near, down_near, route),
        20 * mib,
        scratch=[
            VMEM((rows, width), bf16),
            VMEM((rows, hidden_units), f32),
            VMEM((rows, hidden_units), f32),
            VMEM((rows, hidden_units), bf16),
        ],
    )
    came = lax.ppermute(sent, "wide", swap)
    pairs_sum = call(add_kernel, shaped((chips, q_dev, width), bf16), (own, came), 16 * mib)
    parts = exchange(pairs_sum, groups)
    queries = call(
        embed_kernel,
        shaped((n, capacity, width + LANES), bf16),
        (parts, hidden_in, final_gain[None], route),
        16 * mib,
        cost=ahead(codes),
    )
    recv = exchange(queries)
    scores = call(
        score_kernel,
        shaped((n, capacity, list_rows), f32),
        (recv, codes_near, jnp.swapaxes(scales, 1, 2)),
        20 * mib,
        scratch=[VMEM((2 * n * capacity, width), bf16)],
    )
    back = exchange(scores)
    return call(best_kernel, shaped((q_dev, K_TOP), f32), (back, route), 8 * mib)


def solution(mesh):
    in_specs = (
        P(("grp", "wide"), None),
        P(),
        P(None, "wide"),
        P(None, "wide"),
        P("wide", None),
        P(),
        P(("grp", "wide"), None, None),
        P(("grp", "wide"), None, None),
        P("grp"),
        P("grp"),
        P(("grp", "wide"), None),
    )
    out_specs = P(("grp", "wide"), None)
    return jax.shard_map(body, mesh=mesh, in_specs=in_specs, out_specs=out_specs, check_vma=False)
```

```python
import functools

import jax
import jax.numpy as jnp
from jax import lax
from jax.experimental import pallas as pl
from jax.experimental.pallas import tpu as pltpu
from jax.sharding import PartitionSpec as P

PROBES = 8
K_TOP = 8
BLOCK = 128
LANES = 128

floor_score = -1e30

VMEM = pltpu.VMEM


def call(kernel, out_shape, args, vmem, cost=None, scratch=()):
    many = isinstance(out_shape, (list, tuple))
    return pl.pallas_call(
        kernel,
        out_shape=out_shape,
        in_specs=[pl.BlockSpec(memory_space=VMEM)] * len(args),
        out_specs=[pl.BlockSpec(memory_space=VMEM)] * len(out_shape)
        if many
        else pl.BlockSpec(memory_space=VMEM),
        scratch_shapes=list(scratch),
        compiler_params=pltpu.CompilerParams(vmem_limit_bytes=vmem),
        cost_estimate=cost,
    )(*args)


def ahead(*arrays):
    total = sum(a.size * a.dtype.itemsize for a in arrays)
    return pl.CostEstimate(flops=1000 * total, bytes_accessed=1 << 20, transcendentals=0)


def products(count):
    return pl.CostEstimate(flops=2 * count, bytes_accessed=1 << 20, transcendentals=0)


def shaped(shape, dtype):
    return jax.ShapeDtypeStruct(shape, dtype)


def norm_kernel(hidden_ref, gain_ref, out_ref, rows_ref, scale_ref, sems):
    rows_copy = pltpu.make_async_copy(hidden_ref, rows_ref, sems.at[0])
    gain_copy = pltpu.make_async_copy(gain_ref, scale_ref, sems.at[1])
    rows_copy.start()
    gain_copy.start()
    rows_copy.wait()
    gain_copy.wait()
    rows = rows_ref[...].astype(jnp.float32)
    scale = lax.rsqrt(jnp.mean(rows * rows, axis=-1, keepdims=True) + 1e-05)
    out_ref[...] = (rows * scale * scale_ref[...]).astype(jnp.bfloat16)


def spread_kernel(normed_ref, out_ref):
    half = out_ref.shape[2]
    for k in range(out_ref.shape[0]):
        core = k % 2
        out_ref[k] = normed_ref[:, core * half : (core + 1) * half]


def route_kernel(lists_dev, capacity, probes_ref, slot_ref, count_ref, after_ref, out_ref):
    q_dev, probes = probes_ref.shape
    lists = slot_ref.shape[1]
    pairs = q_dev * probes
    slots = out_ref.shape[0]
    ids = jnp.concatenate(
        [jnp.broadcast_to(probes_ref[q : q + 1, :], (probes, probes)) for q in range(q_dev)], axis=0
    )
    sub = lax.broadcasted_iota(jnp.int32, (pairs, probes), 0)
    lane = lax.broadcasted_iota(jnp.int32, (pairs, probes), 1)
    ids = jnp.sum(jnp.where(sub % probes == lane, ids, 0), axis=1, keepdims=True)
    hit = lax.broadcasted_iota(jnp.int32, (pairs, lists), 1) == ids
    slot = jnp.sum(jnp.where(hit, slot_ref[...], 0), axis=1, keepdims=True)
    valid = jnp.sum(jnp.where(hit, count_ref[...], 0), axis=1, keepdims=True)
    owner = slot // lists_dev
    local = slot % lists_dev
    p_sub = lax.broadcasted_iota(jnp.int32, (pairs, pairs), 0)
    p_lane = lax.broadcasted_iota(jnp.int32, (pairs, pairs), 1)
    diagonal = p_sub == p_lane

    def as_row(column):
        return jnp.sum(jnp.where(diagonal, column, 0), axis=0, keepdims=True)

    owner_row = as_row(owner)
    rank_row = jnp.sum(
        jnp.where((owner == owner_row) & (p_sub < p_lane), 1, 0), axis=0, keepdims=True
    )
    target_row = owner_row * capacity + rank_row
    here = lax.broadcasted_iota(jnp.int32, (slots, pairs), 0) == target_row
    pair_row = lax.broadcasted_iota(jnp.int32, (slots, pairs), 1)

    def of_slot(row):
        return jnp.sum(jnp.where(here, row, 0), axis=1, keepdims=True)

    query = of_slot(pair_row // probes + 1) - 1
    place = lax.broadcasted_iota(jnp.int32, (slots, LANES), 1)
    out = jnp.where(place == 0, query, 0)
    out = jnp.where(place == 1, of_slot(as_row(local)), out)
    out_ref[...] = jnp.where(place == 2, of_slot(as_row(valid)), out)


def half_span(mine, half):
    core = lax.rem(lax.axis_index("wide"), 2)
    which = core if mine else 1 - core
    return pl.ds(pl.multiple_of(which * half, half), half)


def first_kernel(here_ref, gate_ref, up_ref, after_ref, gate_out, up_out, rows_ref):
    rows_ref[...] = here_ref[...].reshape(rows_ref.shape)
    span = half_span(True, rows_ref.shape[1])
    gate_out[...] = jnp.dot(rows_ref[...], gate_ref[span, :], preferred_element_type=jnp.float32)
    up_out[...] = jnp.dot(rows_ref[...], up_ref[span, :], preferred_element_type=jnp.float32)


def second_kernel(
    there_ref, gate_part, up_part, gate_ref, up_ref, down_ref, after_ref, act_ref, send_ref, rows_ref
):
    half = rows_ref.shape[1]
    rows_ref[...] = there_ref[...].reshape(rows_ref.shape)
    span = half_span(False, half)
    gate = gate_part[...] + jnp.dot(
        rows_ref[...], gate_ref[span, :], preferred_element_type=jnp.float32
    )
    up = up_part[...] + jnp.dot(
        rows_ref[...], up_ref[span, :], preferred_element_type=jnp.float32
    )
    act_ref[...] = (gate / (1.0 + jnp.exp(-gate)) * up).astype(jnp.bfloat16)
    send_ref[...] = jnp.dot(
        act_ref[...], down_ref[:, span], preferred_element_type=jnp.float32
    ).astype(jnp.bfloat16)


def third_kernel(act_ref, down_ref, own_ref):
    span = half_span(True, own_ref.shape[1])
    own_ref[...] = jnp.dot(act_ref[...], down_ref[:, span], preferred_element_type=jnp.float32)


def add_kernel(own_ref, came_ref, out_ref):
    total = own_ref[...] + came_ref[...].astype(jnp.float32)
    out_ref[...] = total.astype(jnp.bfloat16).reshape(out_ref.shape)


def embed_kernel(parts_ref, hidden_ref, gain_ref, route_ref, out_ref):
    devices, q_dev, half = parts_ref.shape
    width = 2 * half
    totals = [parts_ref[core].astype(jnp.float32) for core in range(2)]
    for k in range(2, devices):
        totals[k % 2] += parts_ref[k].astype(jnp.float32)
    total = jnp.concatenate(totals, axis=1)
    scaled = gain_ref[...] * (hidden_ref[...].astype(jnp.float32) + total)
    embedded = scaled * lax.rsqrt(jnp.sum(scaled * scaled, axis=-1, keepdims=True) + 1e-06)
    query = route_ref[:, 0:1]
    sent = jnp.zeros((query.shape[0], width), jnp.float32)
    for q in range(q_dev):
        sent = jnp.where(query == q, embedded[q : q + 1, :], sent)
    out_ref[:, :, :width] = sent.astype(jnp.bfloat16).reshape(out_ref.shape[:2] + (width,))
    lane = lax.broadcasted_iota(jnp.int32, (query.shape[0], LANES), 1)
    local = jnp.where(lane == 0, route_ref[:, 1:2], 0).astype(jnp.float32)
    out_ref[:, :, width:] = local.astype(jnp.bfloat16).reshape(out_ref.shape[:2] + (LANES,))


def score_kernel(came_ref, codes_ref, scales_ref, out_ref, rows_ref):
    sources, slots, _ = came_ref.shape
    lists, list_rows, width = codes_ref.shape
    pairs = sources * slots
    came = came_ref[...].reshape(pairs, width + LANES)
    nothing = jnp.zeros((pairs, BLOCK), jnp.bfloat16)
    for block in range(width // BLOCK):
        span = slice(block * BLOCK, (block + 1) * BLOCK)
        kept = block % 2
        rows_ref[kept * pairs : (kept + 1) * pairs, span] = came[:, span]
        rows_ref[(1 - kept) * pairs : (2 - kept) * pairs, span] = nothing
    local = came[:, width : width + 1].astype(jnp.float32).astype(jnp.int32)

    picked = jnp.zeros((pairs, list_rows), jnp.float32)
    for first in range(0, lists, 2):
        scale = jnp.concatenate([scales_ref[first], scales_ref[first + 1]], axis=1)
        total = jnp.zeros((pairs, 2 * list_rows), jnp.float32)
        for step in range(width // (2 * BLOCK)):
            span = slice(step * 2 * BLOCK, (step + 1) * 2 * BLOCK)
            part = lax.dot_general(
                rows_ref[:, span],
                codes_ref[first : first + 2, :, span].reshape(2 * list_rows, 2 * BLOCK),
                (((1,), (1,)), ((), ())),
                preferred_element_type=jnp.float32,
            )
            total += part[:pairs] * scale[2 * step : 2 * step + 1, :]
            total += part[pairs:] * scale[2 * step + 1 : 2 * step + 2, :]
        picked = jnp.where(local == first, total[:, :list_rows], picked)
        picked = jnp.where(local == first + 1, total[:, list_rows:], picked)
    out_ref[...] = picked.reshape(out_ref.shape)


def best_kernel(back_ref, route_ref, out_ref):
    q_dev, count = out_ref.shape
    sources, slots, list_rows = back_ref.shape
    pairs = sources * slots
    scores = back_ref[...].reshape(pairs, list_rows)
    query = route_ref[:, 0:1]
    alive = lax.broadcasted_iota(jnp.int32, (pairs, list_rows), 1) < route_ref[:, 2:3]
    left = jnp.concatenate(
        [jnp.where(alive & (query == q), scores, floor_score)[None] for q in range(q_dev)], axis=0
    )
    column = lax.broadcasted_iota(jnp.int32, (q_dev, count), 1)
    best = jnp.zeros((q_dev, count), jnp.float32)
    filled = jnp.zeros((q_dev, 1), jnp.float32)
    for rank in range(count):
        top = jnp.max(jnp.max(left, axis=1), axis=-1, keepdims=True)
        best = jnp.where(column >= filled.astype(jnp.int32), top, best)
        if rank + 1 < count:
            same = left == top[:, :, None]
            filled += jnp.sum(
                jnp.sum(jnp.where(same, 1.0, 0.0), axis=1), axis=-1, keepdims=True
            )
            left = jnp.where(same, floor_score * 2, left)
    out_ref[...] = best


def body(
    hidden_in,
    ffn_gain,
    gate_weight,
    up_weight,
    down_weight,
    final_gain,
    codes,
    scales,
    counts,
    list_slot,
    probes,
):
    q_dev, width = hidden_in.shape
    hidden_units = gate_weight.shape[1]
    n = lax.axis_size("wide")
    half = width // 2
    rows = n * q_dev
    lists_dev, list_rows, _ = codes.shape
    capacity = (q_dev * PROBES + n - 1) // n
    swap = [(i, i ^ 1) for i in range(n)]
    mib = 1 << 20
    f32, bf16 = jnp.float32, jnp.bfloat16

    def exchange(x):
        return lax.all_to_all(x, "wide", 0, 0, tiled=True)

    gate_near = pltpu.with_memory_space_constraint(gate_weight, VMEM)
    up_near = pltpu.with_memory_space_constraint(up_weight, VMEM)
    down_near = pltpu.with_memory_space_constraint(down_weight, VMEM)
    codes_near = pltpu.with_memory_space_constraint(codes, VMEM)

    normed = pl.pallas_call(
        norm_kernel,
        out_shape=shaped((q_dev, width), bf16),
        in_specs=[pl.BlockSpec(memory_space=pltpu.HBM)] * 2,
        out_specs=pl.BlockSpec(memory_space=VMEM),
        scratch_shapes=[
            VMEM((q_dev, width), bf16),
            VMEM((1, width), f32),
            pltpu.SemaphoreType.DMA((2,)),
        ],
        compiler_params=pltpu.CompilerParams(vmem_limit_bytes=8 * mib),
    )(
        pltpu.with_memory_space_constraint(hidden_in, pltpu.HBM),
        pltpu.with_memory_space_constraint(ffn_gain[None], pltpu.HBM),
    )
    spread = call(
        spread_kernel,
        shaped((n, q_dev, half), bf16),
        (normed,),
        8 * mib,
        cost=ahead(gate_weight, up_weight, down_weight),
    )
    here = exchange(spread)
    there = lax.ppermute(here, "wide", swap)
    route = call(
        functools.partial(route_kernel, lists_dev, capacity),
        shaped((n * capacity, LANES), jnp.int32),
        (probes, list_slot[None], counts[None], here),
        8 * mib,
    )
    gate_part, up_part = call(
        first_kernel,
        [shaped((rows, hidden_units), f32)] * 2,
        (here, gate_near, up_near, down_near),
        8 * mib,
        cost=products(rows * half * hidden_units * 2),
        scratch=[VMEM((rows, half), bf16)],
    )
    act, sent = call(
        second_kernel,
        [shaped((rows, hidden_units), bf16), shaped((rows, half), bf16)],
        (there, gate_part, up_part, gate_near, up_near, down_near, route),
        8 * mib,
        scratch=[VMEM((rows, half), bf16)],
    )
    came = lax.ppermute(sent, "wide", swap)
    own = call(
        third_kernel,
        shaped((rows, half), f32),
        (act, down_near),
        8 * mib,
        cost=products(rows * half * hidden_units),
    )
    pairs_sum = call(add_kernel, shaped((n, q_dev, half), bf16), (own, came), 16 * mib)
    parts = exchange(pairs_sum)
    queries = call(
        embed_kernel,
        shaped((n, capacity, width + LANES), bf16),
        (parts, hidden_in, final_gain[None], route),
        16 * mib,
        cost=ahead(codes),
    )
    recv = exchange(queries)
    scores = call(
        score_kernel,
        shaped((n, capacity, list_rows), f32),
        (recv, codes_near, jnp.swapaxes(scales, 1, 2)),
        20 * mib,
        scratch=[VMEM((2 * n * capacity, width), bf16)],
    )
    back = exchange(scores)
    return call(best_kernel, shaped((q_dev, K_TOP), f32), (back, route), 8 * mib)


def solution(mesh):
    in_specs = (
        P(("grp", "wide"), None),
        P(),
        P(None, "wide"),
        P(None, "wide"),
        P("wide", None),
        P(),
        P(("grp", "wide"), None, None),
        P(("grp", "wide"), None, None),
        P("grp"),
        P("grp"),
        P(("grp", "wide"), None),
    )
    out_specs = P(("grp", "wide"), None)
    return jax.shard_map(body, mesh=mesh, in_specs=in_specs, out_specs=out_specs, check_vma=False)
```

```python
import functools

import jax
import jax.numpy as jnp
from jax import lax
from jax.experimental import pallas as pl
from jax.experimental.pallas import tpu as pltpu
from jax.sharding import PartitionSpec as P

PROBES = 8
K_TOP = 8
BLOCK = 128
LANES = 128
DIGIT = 256

floor_score = -1e30

VMEM = pltpu.VMEM


def call(kernel, out_shape, args, vmem, cost=None, scratch=()):
    many = isinstance(out_shape, (list, tuple))
    return pl.pallas_call(
        kernel,
        out_shape=out_shape,
        in_specs=[pl.BlockSpec(memory_space=VMEM)] * len(args),
        out_specs=[pl.BlockSpec(memory_space=VMEM)] * len(out_shape)
        if many
        else pl.BlockSpec(memory_space=VMEM),
        scratch_shapes=list(scratch),
        compiler_params=pltpu.CompilerParams(vmem_limit_bytes=vmem),
        cost_estimate=cost,
    )(*args)


def ahead(*arrays):
    total = sum(a.size * a.dtype.itemsize for a in arrays)
    return pl.CostEstimate(flops=1000 * total, bytes_accessed=1 << 20, transcendentals=0)


def products(count):
    return pl.CostEstimate(flops=2 * count, bytes_accessed=1 << 20, transcendentals=0)


def shaped(shape, dtype):
    return jax.ShapeDtypeStruct(shape, dtype)


def norm_kernel(hidden_ref, gain_ref, probes_ref, out_ref, rows_ref, scale_ref, ids_ref, sems):
    copies = [
        pltpu.make_async_copy(source, target, sems.at[index])
        for index, (source, target) in enumerate(
            [(hidden_ref, rows_ref), (gain_ref, scale_ref), (probes_ref, ids_ref)]
        )
    ]
    for copy in copies:
        copy.start()
    for copy in copies:
        copy.wait()
    rows = rows_ref[...].astype(jnp.float32)
    width = rows.shape[1]
    scale = lax.rsqrt(jnp.mean(rows * rows, axis=-1, keepdims=True) + 1e-05)
    out_ref[:, :width] = (rows * scale * scale_ref[...]).astype(jnp.bfloat16)

    q_dev, probes = ids_ref.shape
    pairs = q_dev * probes
    lane = lax.broadcasted_iota(jnp.int32, (q_dev, LANES), 1)
    query = lax.broadcasted_iota(jnp.int32, (q_dev, LANES), 0)
    ids = jnp.zeros((q_dev, LANES), jnp.int32)
    for j in range(probes):
        ids = jnp.where(lane % probes == j, ids_ref[:, j : j + 1], ids)
    ids = jnp.where((lane % pairs) // probes == query, ids, 0)
    ids = jnp.sum(ids, axis=0, keepdims=True)
    digits = jnp.where(lane < pairs, ids // DIGIT, ids % DIGIT)
    digits = jnp.where(lane < 2 * pairs, digits, 0)
    out_ref[:, width:] = digits.astype(jnp.float32).astype(jnp.bfloat16)


def spread_kernel(normed_ref, out_ref):
    half = out_ref.shape[2] - LANES
    for k in range(out_ref.shape[0]):
        core = k % 2
        out_ref[k, :, :half] = normed_ref[:, core * half : (core + 1) * half]
        out_ref[k, :, half:] = normed_ref[:, 2 * half :]


def wanted_kernel(capacity, q_dev, probes, here_ref, slot_ref, after_ref, out_ref):
    devices, _, wide = here_ref.shape
    half = wide - LANES
    lists = slot_ref.shape[1]
    pairs = q_dev * probes
    lists_dev = lists // devices
    me = lax.axis_index("wide")
    tails = here_ref[:, :, half:].astype(jnp.float32)
    tails = jnp.max(tails, axis=1).astype(jnp.int32)
    ids = tails[:, :pairs] * DIGIT + tails[:, pairs : 2 * pairs]
    number = lax.broadcasted_iota(jnp.int32, (1, lists), 1)
    local = jnp.full((devices, pairs), -1, jnp.int32)
    for index in range(lists_dev):
        held = slot_ref[...] == me * lists_dev + index
        mine = jnp.sum(jnp.where(held, number, 0), axis=1, keepdims=True)
        local = jnp.where(ids == mine, index, local)
    pair = lax.broadcasted_iota(jnp.int32, (devices, pairs), 1)
    home = lax.broadcasted_iota(jnp.int32, (devices, 1), 0)
    place = lax.broadcasted_iota(jnp.int32, (devices, LANES), 1)
    side = lax.rem(me, 4) // 2
    before = jnp.full((devices, 1), -1, jnp.int32)
    for rank in range(capacity):
        open_pair = (local >= 0) & (pair > before)
        chosen = jnp.min(jnp.where(open_pair, pair, pairs), axis=1, keepdims=True)
        there = jnp.sum(jnp.where(pair == chosen, local, 0), axis=1, keepdims=True)
        row = jnp.where(
            lax.rem(home, 4) // 2 == side, 0, devices * q_dev // 2
        ) + home // 4 * (2 * q_dev) + lax.rem(home, 2) * q_dev + chosen // probes
        row = jnp.where(chosen < pairs, row, -1)
        out_ref[rank * devices : (rank + 1) * devices, :] = jnp.where(
            place == 0, row, jnp.where(place == 1, there, 0)
        )
        before = chosen


def route_kernel(lists_dev, capacity, probes_ref, slot_ref, count_ref, after_ref, out_ref):
    q_dev, probes = probes_ref.shape
    lists = slot_ref.shape[1]
    pairs = q_dev * probes
    slots = out_ref.shape[0]
    ids = jnp.concatenate(
        [jnp.broadcast_to(probes_ref[q : q + 1, :], (probes, probes)) for q in range(q_dev)], axis=0
    )
    sub = lax.broadcasted_iota(jnp.int32, (pairs, probes), 0)
    lane = lax.broadcasted_iota(jnp.int32, (pairs, probes), 1)
    ids = jnp.sum(jnp.where(sub % probes == lane, ids, 0), axis=1, keepdims=True)
    hit = lax.broadcasted_iota(jnp.int32, (pairs, lists), 1) == ids
    slot = jnp.sum(jnp.where(hit, slot_ref[...], 0), axis=1, keepdims=True)
    valid = jnp.sum(jnp.where(hit, count_ref[...], 0), axis=1, keepdims=True)
    owner = slot // lists_dev
    local = slot % lists_dev
    p_sub = lax.broadcasted_iota(jnp.int32, (pairs, pairs), 0)
    p_lane = lax.broadcasted_iota(jnp.int32, (pairs, pairs), 1)
    diagonal = p_sub == p_lane

    def as_row(column):
        return jnp.sum(jnp.where(diagonal, column, 0), axis=0, keepdims=True)

    owner_row = as_row(owner)
    rank_row = jnp.sum(
        jnp.where((owner == owner_row) & (p_sub < p_lane), 1, 0), axis=0, keepdims=True
    )
    target_row = owner_row * capacity + rank_row
    here = lax.broadcasted_iota(jnp.int32, (slots, pairs), 0) == target_row
    pair_row = lax.broadcasted_iota(jnp.int32, (slots, pairs), 1)

    def of_slot(row):
        return jnp.sum(jnp.where(here, row, 0), axis=1, keepdims=True)

    query = of_slot(pair_row // probes + 1) - 1
    place = lax.broadcasted_iota(jnp.int32, (slots, LANES), 1)
    out = jnp.where(place == 0, query, 0)
    out = jnp.where(place == 1, of_slot(as_row(local)), out)
    out_ref[...] = jnp.where(place == 2, of_slot(as_row(valid)), out)


def half_span(mine, half):
    core = lax.rem(lax.axis_index("wide"), 2)
    which = core if mine else 1 - core
    return pl.ds(pl.multiple_of(which * half, half), half)


def first_kernel(here_ref, gate_ref, up_ref, after_ref, gate_out, up_out, rows_ref):
    rows_ref[...] = here_ref[:, :, : rows_ref.shape[1]].reshape(rows_ref.shape)
    span = half_span(True, rows_ref.shape[1])
    gate_out[...] = jnp.dot(rows_ref[...], gate_ref[span, :], preferred_element_type=jnp.float32)
    up_out[...] = jnp.dot(rows_ref[...], up_ref[span, :], preferred_element_type=jnp.float32)


def second_kernel(
    there_ref, gate_part, up_part, gate_ref, up_ref, down_ref, hidden_ref, act_ref, send_ref, rows_ref
):
    half = rows_ref.shape[1]
    rows_ref[...] = there_ref[:, :, :half].reshape(rows_ref.shape)
    span = half_span(False, half)
    gate = gate_part[...] + jnp.dot(
        rows_ref[...], gate_ref[span, :], preferred_element_type=jnp.float32
    )
    up = up_part[...] + jnp.dot(
        rows_ref[...], up_ref[span, :], preferred_element_type=jnp.float32
    )
    act_ref[...] = (gate / (1.0 + jnp.exp(-gate)) * up).astype(jnp.bfloat16)
    rows = act_ref.shape[0]
    send_ref[:rows, :] = jnp.dot(
        act_ref[...], down_ref[:, span], preferred_element_type=jnp.float32
    ).astype(jnp.bfloat16)
    residual = hidden_ref[:, span]
    send_ref[rows:, :] = jnp.concatenate([residual, residual], axis=0)


def third_kernel(act_ref, down_ref, own_ref):
    span = half_span(True, own_ref.shape[1])
    own_ref[...] = jnp.dot(act_ref[...], down_ref[:, span], preferred_element_type=jnp.float32)


def side_kernel(own_ref, came_ref, hidden_ref, keep_ref, send_ref):
    rows, half = own_ref.shape
    q_dev = hidden_ref.shape[0]
    me = lax.axis_index("wide")
    core, side, plane = lax.rem(me, 2), lax.rem(me, 4) // 2, me // 4
    group = 2 * q_dev
    mine = jnp.where(core == 0, hidden_ref[:, :half], hidden_ref[:, half:]).astype(jnp.float32)
    other = came_ref[rows : rows + q_dev, :].astype(jnp.float32)
    residual = jnp.where(
        core == 0,
        jnp.concatenate([mine, other], axis=0),
        jnp.concatenate([other, mine], axis=0),
    )
    for z in range(rows // (2 * group)):
        total = []
        for y in range(2):
            span = slice((2 * z + y) * group, (2 * z + y + 1) * group)
            total.append(own_ref[span, :] + came_ref[span, :].astype(jnp.float32))
        kept = jnp.where(side == 0, total[0], total[1])
        sent = jnp.where(side == 0, total[1], total[0])
        span = slice(z * group, (z + 1) * group)
        keep_ref[span, :] = kept + jnp.where(plane == z, residual, jnp.zeros_like(residual))
        send_ref[span, :] = sent.astype(jnp.bfloat16)


def sum_kernel(keep_ref, came_ref, after_ref, total_ref, send_ref):
    total = keep_ref[...] + came_ref[...].astype(jnp.float32)
    total_ref[...] = total
    send_ref[...] = total.astype(jnp.bfloat16)


def scale_kernel(keep_ref, came_ref, gain_ref, out_ref):
    rows, half = keep_ref.shape
    core = lax.rem(lax.axis_index("wide"), 2)
    gain = jnp.where(core == 0, gain_ref[:, :half], gain_ref[:, half:])
    scaled = gain * (keep_ref[...] + came_ref[...].astype(jnp.float32))
    out_ref[:, :half] = scaled.astype(jnp.bfloat16)
    left = jnp.sum(scaled * scaled, axis=-1, keepdims=True)
    lane = lax.broadcasted_iota(jnp.int32, (rows, LANES), 1)
    tail = jnp.zeros((rows, LANES), jnp.float32)
    for piece in range(3):
        part = left.astype(jnp.bfloat16).astype(jnp.float32)
        tail = jnp.where(lane == piece, part, tail)
        left = left - part
    out_ref[:, half:] = tail.astype(jnp.bfloat16)


def half_scores(mine, near_ref, far_ref, wanted_ref, codes_ref, scales_ref, picks_ref, rows_ref):
    side_rows, wide = near_ref.shape
    half = wide - LANES
    lists, list_rows, _ = codes_ref.shape
    pairs = wanted_ref.shape[0]
    core = lax.rem(lax.axis_index("wide"), 2)
    which = core if mine else 1 - core
    row = wanted_ref[:, 0:1]
    local = wanted_ref[:, 1:2]
    column = lax.broadcasted_iota(jnp.int32, (pairs, side_rows), 1)

    def pick(ref, first):
        hot = jnp.where(column + first == row, 1.0, 0.0).astype(jnp.bfloat16)
        return jnp.dot(hot, ref[...], preferred_element_type=jnp.float32)

    chosen = pick(near_ref, 0) + pick(far_ref, side_rows)
    picks_ref[...] = chosen.astype(jnp.bfloat16)
    nothing = jnp.zeros((pairs, BLOCK), jnp.bfloat16)
    for block in range(half // BLOCK):
        span = slice(block * BLOCK, (block + 1) * BLOCK)
        kept = block % 2
        rows_ref[kept * pairs : (kept + 1) * pairs, span] = picks_ref[:, span]
        rows_ref[(1 - kept) * pairs : (2 - kept) * pairs, span] = nothing
    squares = jnp.sum(chosen[:, half:], axis=1, keepdims=True)

    blocks = half // BLOCK
    picked = jnp.zeros((pairs, list_rows), jnp.float32)
    here = pl.ds(pl.multiple_of(which * blocks, blocks), blocks)
    for first in range(0, lists, 2):
        scale = jnp.concatenate([scales_ref[first, here, :], scales_ref[first + 1, here, :]], axis=1)
        total = jnp.zeros((pairs, 2 * list_rows), jnp.float32)
        for step in range(blocks // 2):
            span = slice(step * 2 * BLOCK, (step + 1) * 2 * BLOCK)
            away = pl.ds(pl.multiple_of(which * half + step * 2 * BLOCK, 2 * BLOCK), 2 * BLOCK)
            part = lax.dot_general(
                rows_ref[:, span],
                codes_ref[first : first + 2, :, away].reshape(2 * list_rows, 2 * BLOCK),
                (((1,), (1,)), ((), ())),
                preferred_element_type=jnp.float32,
            )
            total += part[:pairs] * scale[2 * step : 2 * step + 1, :]
            total += part[pairs:] * scale[2 * step + 1 : 2 * step + 2, :]
        picked = jnp.where(local == first, total[:, :list_rows], picked)
        picked = jnp.where(local == first + 1, total[:, list_rows:], picked)
    return picked, squares


def near_scores_kernel(
    near_ref, far_ref, wanted_ref, codes_ref, scales_ref, picked_ref, squares_ref, picks_ref, rows_ref
):
    picked, squares = half_scores(
        True, near_ref, far_ref, wanted_ref, codes_ref, scales_ref, picks_ref, rows_ref
    )
    picked_ref[...] = picked
    squares_ref[...] = jnp.broadcast_to(squares, squares_ref.shape)


def scores_kernel(
    near_ref, far_ref, wanted_ref, codes_ref, scales_ref, picked_ref, squares_ref, out_ref,
    picks_ref, rows_ref,
):
    picked, squares = half_scores(
        False, near_ref, far_ref, wanted_ref, codes_ref, scales_ref, picks_ref, rows_ref
    )
    scale = lax.rsqrt(squares_ref[:, 0:1] + squares + 1e-06)
    scores = (picked_ref[...] + picked) * scale
    devices, capacity, _ = out_ref.shape
    for rank in range(capacity):
        out_ref[:, rank, :] = scores[rank * devices : (rank + 1) * devices]


def best_kernel(back_ref, route_ref, out_ref):
    q_dev, count = out_ref.shape
    sources, slots, list_rows = back_ref.shape
    pairs = sources * slots
    scores = back_ref[...].reshape(pairs, list_rows)
    query = route_ref[:, 0:1]
    alive = lax.broadcasted_iota(jnp.int32, (pairs, list_rows), 1) < route_ref[:, 2:3]
    left = jnp.concatenate(
        [jnp.where(alive & (query == q), scores, floor_score)[None] for q in range(q_dev)], axis=0
    )
    column = lax.broadcasted_iota(jnp.int32, (q_dev, count), 1)
    best = jnp.zeros((q_dev, count), jnp.float32)
    filled = jnp.zeros((q_dev, 1), jnp.float32)
    for rank in range(count):
        top = jnp.max(jnp.max(left, axis=1), axis=-1, keepdims=True)
        best = jnp.where(column >= filled.astype(jnp.int32), top, best)
        if rank + 1 < count:
            same = left == top[:, :, None]
            filled += jnp.sum(
                jnp.sum(jnp.where(same, 1.0, 0.0), axis=1), axis=-1, keepdims=True
            )
            left = jnp.where(same, floor_score * 2, left)
    out_ref[...] = best


def body(
    hidden_in,
    ffn_gain,
    gate_weight,
    up_weight,
    down_weight,
    final_gain,
    codes,
    scales,
    counts,
    list_slot,
    probes,
):
    q_dev, width = hidden_in.shape
    hidden_units = gate_weight.shape[1]
    n = lax.axis_size("wide")
    half = width // 2
    rows = n * q_dev
    lists_dev, list_rows, _ = codes.shape
    capacity = (q_dev * PROBES + n - 1) // n
    mib = 1 << 20
    f32, bf16 = jnp.float32, jnp.bfloat16

    def exchange(x):
        return lax.all_to_all(x, "wide", 0, 0, tiled=True)

    def swapped(x, bit):
        return lax.ppermute(x, "wide", [(i, i ^ bit) for i in range(n)])

    gate_near = pltpu.with_memory_space_constraint(gate_weight, VMEM)
    up_near = pltpu.with_memory_space_constraint(up_weight, VMEM)
    down_near = pltpu.with_memory_space_constraint(down_weight, VMEM)
    codes_near = pltpu.with_memory_space_constraint(codes, VMEM)

    normed = pl.pallas_call(
        norm_kernel,
        out_shape=shaped((q_dev, width + LANES), bf16),
        in_specs=[pl.BlockSpec(memory_space=pltpu.HBM)] * 3,
        out_specs=pl.BlockSpec(memory_space=VMEM),
        scratch_shapes=[
            VMEM((q_dev, width), bf16),
            VMEM((1, width), f32),
            VMEM(probes.shape, jnp.int32),
            pltpu.SemaphoreType.DMA((3,)),
        ],
        compiler_params=pltpu.CompilerParams(vmem_limit_bytes=8 * mib),
    )(
        pltpu.with_memory_space_constraint(hidden_in, pltpu.HBM),
        pltpu.with_memory_space_constraint(ffn_gain[None], pltpu.HBM),
        pltpu.with_memory_space_constraint(probes, pltpu.HBM),
    )
    spread = call(
        spread_kernel,
        shaped((n, q_dev, half + LANES), bf16),
        (normed,),
        8 * mib,
        cost=ahead(gate_weight, up_weight, down_weight),
    )
    here = exchange(spread)
    there = swapped(here, 1)
    gate_part, up_part = call(
        first_kernel,
        [shaped((rows, hidden_units), f32)] * 2,
        (here, gate_near, up_near, down_near),
        8 * mib,
        cost=products(rows * half * hidden_units * 2),
        scratch=[VMEM((rows, half), bf16)],
    )
    act, sent = call(
        second_kernel,
        [shaped((rows, hidden_units), bf16), shaped((rows + 2 * q_dev, half), bf16)],
        (there, gate_part, up_part, gate_near, up_near, down_near, hidden_in),
        8 * mib,
        scratch=[VMEM((rows, half), bf16)],
    )
    came = swapped(sent, 1)
    own = call(
        third_kernel,
        shaped((rows, half), f32),
        (act, down_near),
        8 * mib,
        cost=products(rows * half * hidden_units),
    )
    side_rows = rows // 2
    keep, sent = call(
        side_kernel,
        [shaped((side_rows, half), f32), shaped((side_rows, half), bf16)],
        (own, came, hidden_in),
        8 * mib,
    )
    route = call(
        functools.partial(route_kernel, lists_dev, capacity),
        shaped((n * capacity, LANES), jnp.int32),
        (probes, list_slot[None], counts[None], keep),
        4 * mib,
    )
    wanted = call(
        functools.partial(wanted_kernel, capacity, q_dev, PROBES),
        shaped((n * capacity, LANES), jnp.int32),
        (here, list_slot[None], route),
        4 * mib,
    )
    came = swapped(sent, 2)
    bit = 4
    while bit < n:
        keep, sent = call(
            sum_kernel,
            [shaped((side_rows, half), f32), shaped((side_rows, half), bf16)],
            (keep, came, wanted),
            8 * mib,
            cost=ahead(codes) if bit == 4 else None,
        )
        came = swapped(sent, bit)
        bit *= 2
    near = call(
        scale_kernel,
        shaped((side_rows, half + LANES), bf16),
        (keep, came, final_gain[None]),
        8 * mib,
    )
    far = swapped(near, 2)
    near_other = swapped(near, 1)
    far_other = swapped(far, 1)
    scales_near = jnp.swapaxes(scales, 1, 2)
    scratch = [
        VMEM((n * capacity, half + LANES), bf16),
        VMEM((2 * n * capacity, half), bf16),
    ]
    picked, squares = call(
        near_scores_kernel,
        [shaped((n * capacity, list_rows), f32), shaped((n * capacity, LANES), f32)],
        (near, far, wanted, codes_near, scales_near),
        8 * mib,
        cost=products(n * capacity * lists_dev * list_rows * width),
        scratch=scratch,
    )
    scores = call(
        scores_kernel,
        shaped((n, capacity, list_rows), f32),
        (near_other, far_other, wanted, codes_near, scales_near, picked, squares),
        8 * mib,
        scratch=scratch,
    )
    back = exchange(scores)
    return call(best_kernel, shaped((q_dev, K_TOP), f32), (back, route), 8 * mib)


def solution(mesh):
    in_specs = (
        P(("grp", "wide"), None),
        P(),
        P(None, "wide"),
        P(None, "wide"),
        P("wide", None),
        P(),
        P(("grp", "wide"), None, None),
        P(("grp", "wide"), None, None),
        P("grp"),
        P("grp"),
        P(("grp", "wide"), None),
    )
    out_specs = P(("grp", "wide"), None)
    return jax.shard_map(body, mesh=mesh, in_specs=in_specs, out_specs=out_specs, check_vma=False)
```

```python
import functools

import jax
import jax.numpy as jnp
from jax import lax
from jax.experimental import pallas as pl
from jax.experimental.pallas import tpu as pltpu
from jax.sharding import PartitionSpec as P

PROBES = 8
K_TOP = 8
BLOCK = 128
LANES = 128
DIGIT = 256
CHUNKS = 2


floor_score = -1e30

VMEM = pltpu.VMEM


def call(kernel, out_shape, args, vmem, cost=None, scratch=()):
    many = isinstance(out_shape, (list, tuple))
    return pl.pallas_call(
        kernel,
        out_shape=out_shape,
        in_specs=[pl.BlockSpec(memory_space=VMEM)] * len(args),
        out_specs=[pl.BlockSpec(memory_space=VMEM)] * len(out_shape)
        if many
        else pl.BlockSpec(memory_space=VMEM),
        scratch_shapes=list(scratch),
        compiler_params=pltpu.CompilerParams(vmem_limit_bytes=vmem),
        cost_estimate=cost,
    )(*args)


def ahead(*arrays):
    total = sum(a.size * a.dtype.itemsize for a in arrays)
    return pl.CostEstimate(flops=1000 * total, bytes_accessed=1 << 20, transcendentals=0)


def products(count):
    return pl.CostEstimate(flops=2 * count, bytes_accessed=1 << 20, transcendentals=0)


def shaped(shape, dtype):
    return jax.ShapeDtypeStruct(shape, dtype)


def norm_kernel(hidden_ref, gain_ref, probes_ref, out_ref, rows_ref, scale_ref, ids_ref, sems):
    copies = [
        pltpu.make_async_copy(source, target, sems.at[index])
        for index, (source, target) in enumerate(
            [(hidden_ref, rows_ref), (gain_ref, scale_ref), (probes_ref, ids_ref)]
        )
    ]
    for copy in copies:
        copy.start()
    for copy in copies:
        copy.wait()
    rows = rows_ref[...].astype(jnp.float32)
    width = rows.shape[1]
    scale = lax.rsqrt(jnp.mean(rows * rows, axis=-1, keepdims=True) + 1e-05)
    out_ref[:, :width] = (rows * scale * scale_ref[...]).astype(jnp.bfloat16)

    q_dev, probes = ids_ref.shape
    pairs = q_dev * probes
    lane = lax.broadcasted_iota(jnp.int32, (q_dev, LANES), 1)
    query = lax.broadcasted_iota(jnp.int32, (q_dev, LANES), 0)
    ids = jnp.zeros((q_dev, LANES), jnp.int32)
    for j in range(probes):
        ids = jnp.where(lane % probes == j, ids_ref[:, j : j + 1], ids)
    ids = jnp.where((lane % pairs) // probes == query, ids, 0)
    ids = jnp.sum(ids, axis=0, keepdims=True)
    digits = jnp.where(lane < pairs, ids // DIGIT, ids % DIGIT)
    digits = jnp.where(lane < 2 * pairs, digits, 0)
    out_ref[:, width:] = digits.astype(jnp.float32).astype(jnp.bfloat16)


def spread_kernel(normed_ref, out_ref):
    half = out_ref.shape[2] - LANES
    for k in range(out_ref.shape[0]):
        core = k % 2
        out_ref[k, :, :half] = normed_ref[:, core * half : (core + 1) * half]
        out_ref[k, :, half:] = normed_ref[:, 2 * half :]


def wanted_kernel(capacity, q_dev, probes, here_ref, slot_ref, after_ref, out_ref):
    devices, _, wide = here_ref.shape
    half = wide - LANES
    lists = slot_ref.shape[1]
    pairs = q_dev * probes
    lists_dev = lists // devices
    me = lax.axis_index("wide")
    tails = here_ref[:, :, half:].astype(jnp.float32)
    tails = jnp.max(tails, axis=1).astype(jnp.int32)
    ids = tails[:, :pairs] * DIGIT + tails[:, pairs : 2 * pairs]
    number = lax.broadcasted_iota(jnp.int32, (1, lists), 1)
    local = jnp.full((devices, pairs), -1, jnp.int32)
    for index in range(lists_dev):
        held = slot_ref[...] == me * lists_dev + index
        mine = jnp.sum(jnp.where(held, number, 0), axis=1, keepdims=True)
        local = jnp.where(ids == mine, index, local)
    pair = lax.broadcasted_iota(jnp.int32, (devices, pairs), 1)
    home = lax.broadcasted_iota(jnp.int32, (devices, 1), 0)
    place = lax.broadcasted_iota(jnp.int32, (devices, LANES), 1)
    side = lax.rem(me, 4) // 2
    before = jnp.full((devices, 1), -1, jnp.int32)
    for rank in range(capacity):
        open_pair = (local >= 0) & (pair > before)
        chosen = jnp.min(jnp.where(open_pair, pair, pairs), axis=1, keepdims=True)
        there = jnp.sum(jnp.where(pair == chosen, local, 0), axis=1, keepdims=True)
        row = jnp.where(
            lax.rem(home, 4) // 2 == side, 0, devices * q_dev // 2
        ) + home // 4 * (2 * q_dev) + lax.rem(home, 2) * q_dev + chosen // probes
        row = jnp.where(chosen < pairs, row, -1)
        out_ref[rank * devices : (rank + 1) * devices, :] = jnp.where(
            place == 0, row, jnp.where(place == 1, there, 0)
        )
        before = chosen


def route_kernel(lists_dev, capacity, probes_ref, slot_ref, count_ref, after_ref, out_ref):
    q_dev, probes = probes_ref.shape
    lists = slot_ref.shape[1]
    pairs = q_dev * probes
    slots = out_ref.shape[0]
    ids = jnp.concatenate(
        [jnp.broadcast_to(probes_ref[q : q + 1, :], (probes, probes)) for q in range(q_dev)], axis=0
    )
    sub = lax.broadcasted_iota(jnp.int32, (pairs, probes), 0)
    lane = lax.broadcasted_iota(jnp.int32, (pairs, probes), 1)
    ids = jnp.sum(jnp.where(sub % probes == lane, ids, 0), axis=1, keepdims=True)
    hit = lax.broadcasted_iota(jnp.int32, (pairs, lists), 1) == ids
    slot = jnp.sum(jnp.where(hit, slot_ref[...], 0), axis=1, keepdims=True)
    valid = jnp.sum(jnp.where(hit, count_ref[...], 0), axis=1, keepdims=True)
    owner = slot // lists_dev
    local = slot % lists_dev
    p_sub = lax.broadcasted_iota(jnp.int32, (pairs, pairs), 0)
    p_lane = lax.broadcasted_iota(jnp.int32, (pairs, pairs), 1)
    diagonal = p_sub == p_lane

    def as_row(column):
        return jnp.sum(jnp.where(diagonal, column, 0), axis=0, keepdims=True)

    owner_row = as_row(owner)
    rank_row = jnp.sum(
        jnp.where((owner == owner_row) & (p_sub < p_lane), 1, 0), axis=0, keepdims=True
    )
    target_row = owner_row * capacity + rank_row
    here = lax.broadcasted_iota(jnp.int32, (slots, pairs), 0) == target_row
    pair_row = lax.broadcasted_iota(jnp.int32, (slots, pairs), 1)

    def of_slot(row):
        return jnp.sum(jnp.where(here, row, 0), axis=1, keepdims=True)

    query = of_slot(pair_row // probes + 1) - 1
    place = lax.broadcasted_iota(jnp.int32, (slots, LANES), 1)
    out = jnp.where(place == 0, query, 0)
    out = jnp.where(place == 1, of_slot(as_row(local)), out)
    out_ref[...] = jnp.where(place == 2, of_slot(as_row(valid)), out)


def my_span(mine, half, start, size):
    core = lax.rem(lax.axis_index("wide"), 2)
    which = core if mine else 1 - core
    return pl.ds(pl.multiple_of(which * half + start, size), size)


def first_kernel(here_ref, gate_ref, up_ref, after_ref, gate_out, up_out, rows_ref):
    rows_ref[...] = here_ref[:, :, : rows_ref.shape[1]].reshape(rows_ref.shape)
    half = rows_ref.shape[1]
    span = my_span(True, half, 0, half)
    gate_out[...] = jnp.dot(rows_ref[...], gate_ref[span, :], preferred_element_type=jnp.float32)
    up_out[...] = jnp.dot(rows_ref[...], up_ref[span, :], preferred_element_type=jnp.float32)


def put_share(act_ref, down_ref, hidden_ref, send_ref, half, start):
    rows, size = act_ref.shape[0], send_ref.shape[1]
    span = my_span(False, half, start, size)
    send_ref[:rows, :] = jnp.dot(
        act_ref[...], down_ref[:, span], preferred_element_type=jnp.float32
    ).astype(jnp.bfloat16)
    residual = hidden_ref[:, span]
    send_ref[rows:, :] = jnp.concatenate([residual, residual], axis=0)


def second_kernel(
    there_ref, gate_part, up_part, gate_ref, up_ref, down_ref, hidden_ref, act_ref, send_ref, rows_ref
):
    half = rows_ref.shape[1]
    rows_ref[...] = there_ref[:, :, :half].reshape(rows_ref.shape)
    span = my_span(False, half, 0, half)
    gate = gate_part[...] + jnp.dot(
        rows_ref[...], gate_ref[span, :], preferred_element_type=jnp.float32
    )
    up = up_part[...] + jnp.dot(
        rows_ref[...], up_ref[span, :], preferred_element_type=jnp.float32
    )
    act_ref[...] = (gate / (1.0 + jnp.exp(-gate)) * up).astype(jnp.bfloat16)
    put_share(act_ref, down_ref, hidden_ref, send_ref, half, 0)


def share_kernel(half, start, act_ref, down_ref, hidden_ref, send_ref):
    put_share(act_ref, down_ref, hidden_ref, send_ref, half, start)


def own_kernel(half, start, act_ref, down_ref, own_ref):
    span = my_span(True, half, start, own_ref.shape[1])
    own_ref[...] = jnp.dot(act_ref[...], down_ref[:, span], preferred_element_type=jnp.float32)


def side_kernel(start, own_ref, came_ref, hidden_ref, keep_ref, send_ref):
    rows, size = own_ref.shape
    q_dev, width = hidden_ref.shape
    half = width // 2
    me = lax.axis_index("wide")
    core, side, plane = lax.rem(me, 2), lax.rem(me, 4) // 2, me // 4
    group = 2 * q_dev
    mine = jnp.where(
        core == 0,
        hidden_ref[:, start : start + size],
        hidden_ref[:, half + start : half + start + size],
    ).astype(jnp.float32)
    other = came_ref[rows : rows + q_dev, :].astype(jnp.float32)
    residual = jnp.where(
        core == 0,
        jnp.concatenate([mine, other], axis=0),
        jnp.concatenate([other, mine], axis=0),
    )
    for z in range(rows // (2 * group)):
        total = []
        for y in range(2):
            span = slice((2 * z + y) * group, (2 * z + y + 1) * group)
            total.append(own_ref[span, :] + came_ref[span, :].astype(jnp.float32))
        kept = jnp.where(side == 0, total[0], total[1])
        sent = jnp.where(side == 0, total[1], total[0])
        span = slice(z * group, (z + 1) * group)
        keep_ref[span, :] = kept + jnp.where(plane == z, residual, jnp.zeros_like(residual))
        send_ref[span, :] = sent.astype(jnp.bfloat16)


def sum_kernel(keep_ref, came_ref, total_ref, send_ref):
    total = keep_ref[...] + came_ref[...].astype(jnp.float32)
    total_ref[...] = total
    send_ref[...] = total.astype(jnp.bfloat16)


def scale_kernel(start, keep_ref, came_ref, gain_ref, after_ref, out_ref):
    rows, size = keep_ref.shape
    half = gain_ref.shape[1] // 2
    core = lax.rem(lax.axis_index("wide"), 2)
    gain = jnp.where(
        core == 0,
        gain_ref[:, start : start + size],
        gain_ref[:, half + start : half + start + size],
    )
    scaled = gain * (keep_ref[...] + came_ref[...].astype(jnp.float32))
    out_ref[:, :size] = scaled.astype(jnp.bfloat16)
    left = jnp.sum(scaled * scaled, axis=-1, keepdims=True)
    lane = lax.broadcasted_iota(jnp.int32, (rows, LANES), 1)
    tail = jnp.zeros((rows, LANES), jnp.float32)
    for piece in range(3):
        part = left.astype(jnp.bfloat16).astype(jnp.float32)
        tail = jnp.where(lane == piece, part, tail)
        left = left - part
    out_ref[:, size:] = tail.astype(jnp.bfloat16)


def chunk_scores(
    mine, start, near_ref, far_ref, wanted_ref, codes_ref, scales_ref, picks_ref, rows_ref
):
    side_rows, wide = near_ref.shape
    size = wide - LANES
    lists, list_rows, width = codes_ref.shape
    half = width // 2
    pairs = wanted_ref.shape[0]
    row = wanted_ref[:, 0:1]
    local = wanted_ref[:, 1:2]
    column = lax.broadcasted_iota(jnp.int32, (pairs, side_rows), 1)

    def pick(ref, first):
        hot = jnp.where(column + first == row, 1.0, 0.0).astype(jnp.bfloat16)
        return jnp.dot(hot, ref[...], preferred_element_type=jnp.float32)

    chosen = pick(near_ref, 0) + pick(far_ref, side_rows)
    picks_ref[...] = chosen[:, :size].astype(jnp.bfloat16)
    nothing = jnp.zeros((pairs, BLOCK), jnp.bfloat16)
    for block in range(size // BLOCK):
        span = slice(block * BLOCK, (block + 1) * BLOCK)
        kept = block % 2
        rows_ref[kept * pairs : (kept + 1) * pairs, span] = picks_ref[:, span]
        rows_ref[(1 - kept) * pairs : (2 - kept) * pairs, span] = nothing
    squares = jnp.sum(chosen[:, size:], axis=1, keepdims=True)

    core = lax.rem(lax.axis_index("wide"), 2)
    which = core if mine else 1 - core
    blocks = size // BLOCK
    here = pl.ds(
        pl.multiple_of(which * (half // BLOCK) + start // BLOCK, blocks), blocks
    )
    picked = jnp.zeros((pairs, list_rows), jnp.float32)
    for first in range(0, lists, 2):
        scale = jnp.concatenate([scales_ref[first, here, :], scales_ref[first + 1, here, :]], axis=1)
        total = jnp.zeros((pairs, 2 * list_rows), jnp.float32)
        for step in range(blocks // 2):
            span = slice(step * 2 * BLOCK, (step + 1) * 2 * BLOCK)
            away = my_span(mine, half, start + step * 2 * BLOCK, 2 * BLOCK)
            part = lax.dot_general(
                rows_ref[:, span],
                codes_ref[first : first + 2, :, away].reshape(2 * list_rows, 2 * BLOCK),
                (((1,), (1,)), ((), ())),
                preferred_element_type=jnp.float32,
            )
            total += part[:pairs] * scale[2 * step : 2 * step + 1, :]
            total += part[pairs:] * scale[2 * step + 1 : 2 * step + 2, :]
        picked = jnp.where(local == first, total[:, :list_rows], picked)
        picked = jnp.where(local == first + 1, total[:, list_rows:], picked)
    return picked, squares


def some_scores_kernel(
    mine, start, near_ref, far_ref, wanted_ref, codes_ref, scales_ref, *rest
):
    *sofar, picked_ref, squares_ref, picks_ref, rows_ref = rest
    picked, squares = chunk_scores(
        mine, start, near_ref, far_ref, wanted_ref, codes_ref, scales_ref, picks_ref, rows_ref
    )
    if sofar:
        picked += sofar[0][...]
        squares = squares + sofar[1][...]
    picked_ref[...] = picked
    squares_ref[...] = jnp.broadcast_to(squares, squares_ref.shape)


def last_scores_kernel(
    mine, start, near_ref, far_ref, wanted_ref, codes_ref, scales_ref, sofar_ref, squares_ref, out_ref,
    picks_ref, rows_ref,
):
    picked, squares = chunk_scores(
        mine, start, near_ref, far_ref, wanted_ref, codes_ref, scales_ref, picks_ref, rows_ref
    )
    scale = lax.rsqrt(squares_ref[:, 0:1] + squares + 1e-06)
    scores = (sofar_ref[...] + picked) * scale
    devices, capacity, _ = out_ref.shape
    for rank in range(capacity):
        out_ref[:, rank, :] = scores[rank * devices : (rank + 1) * devices]


def best_kernel(back_ref, route_ref, out_ref):
    q_dev, count = out_ref.shape
    sources, slots, list_rows = back_ref.shape
    pairs = sources * slots
    scores = back_ref[...].reshape(pairs, list_rows)
    query = route_ref[:, 0:1]
    alive = lax.broadcasted_iota(jnp.int32, (pairs, list_rows), 1) < route_ref[:, 2:3]
    left = jnp.concatenate(
        [jnp.where(alive & (query == q), scores, floor_score)[None] for q in range(q_dev)], axis=0
    )
    column = lax.broadcasted_iota(jnp.int32, (q_dev, count), 1)
    best = jnp.zeros((q_dev, count), jnp.float32)
    filled = jnp.zeros((q_dev, 1), jnp.float32)
    for rank in range(count):
        top = jnp.max(jnp.max(left, axis=1), axis=-1, keepdims=True)
        best = jnp.where(column >= filled.astype(jnp.int32), top, best)
        if rank + 1 < count:
            same = left == top[:, :, None]
            filled += jnp.sum(
                jnp.sum(jnp.where(same, 1.0, 0.0), axis=1), axis=-1, keepdims=True
            )
            left = jnp.where(same, floor_score * 2, left)
    out_ref[...] = best


def body(
    hidden_in,
    ffn_gain,
    gate_weight,
    up_weight,
    down_weight,
    final_gain,
    codes,
    scales,
    counts,
    list_slot,
    probes,
):
    q_dev, width = hidden_in.shape
    hidden_units = gate_weight.shape[1]
    n = lax.axis_size("wide")
    half = width // 2
    rows = n * q_dev
    lists_dev, list_rows, _ = codes.shape
    capacity = (q_dev * PROBES + n - 1) // n
    mib = 1 << 20
    f32, bf16 = jnp.float32, jnp.bfloat16

    def exchange(x):
        return lax.all_to_all(x, "wide", 0, 0, tiled=True)

    def swapped(x, bit):
        return lax.ppermute(x, "wide", [(i, i ^ bit) for i in range(n)])

    gate_near = pltpu.with_memory_space_constraint(gate_weight, VMEM)
    up_near = pltpu.with_memory_space_constraint(up_weight, VMEM)
    down_near = pltpu.with_memory_space_constraint(down_weight, VMEM)
    codes_near = pltpu.with_memory_space_constraint(codes, VMEM)

    normed = pl.pallas_call(
        norm_kernel,
        out_shape=shaped((q_dev, width + LANES), bf16),
        in_specs=[pl.BlockSpec(memory_space=pltpu.HBM)] * 3,
        out_specs=pl.BlockSpec(memory_space=VMEM),
        scratch_shapes=[
            VMEM((q_dev, width), bf16),
            VMEM((1, width), f32),
            VMEM(probes.shape, jnp.int32),
            pltpu.SemaphoreType.DMA((3,)),
        ],
        compiler_params=pltpu.CompilerParams(vmem_limit_bytes=8 * mib),
    )(
        pltpu.with_memory_space_constraint(hidden_in, pltpu.HBM),
        pltpu.with_memory_space_constraint(ffn_gain[None], pltpu.HBM),
        pltpu.with_memory_space_constraint(probes, pltpu.HBM),
    )
    spread = call(
        spread_kernel,
        shaped((n, q_dev, half + LANES), bf16),
        (normed,),
        8 * mib,
        cost=ahead(gate_weight, up_weight, down_weight),
    )
    here = exchange(spread)
    there = swapped(here, 1)
    gate_part, up_part = call(
        first_kernel,
        [shaped((rows, hidden_units), f32)] * 2,
        (here, gate_near, up_near, down_near),
        8 * mib,
        cost=products(rows * half * hidden_units * 2),
        scratch=[VMEM((rows, half), bf16)],
    )
    size = half // CHUNKS
    starts = [c * size for c in range(CHUNKS)]
    share = shaped((rows + 2 * q_dev, size), bf16)
    act, sent = call(
        second_kernel,
        [shaped((rows, hidden_units), bf16), share],
        (there, gate_part, up_part, gate_near, up_near, down_near, hidden_in),
        8 * mib,
        scratch=[VMEM((rows, half), bf16)],
    )
    came = [swapped(sent, 1)]
    work = products(rows * size * hidden_units)
    for start in starts[1:]:
        sent = call(
            functools.partial(share_kernel, half, start),
            share,
            (act, down_near, hidden_in),
            8 * mib,
            cost=work,
        )
        came.append(swapped(sent, 1))
    side_rows = rows // 2
    kept = [shaped((side_rows, size), f32), shaped((side_rows, size), bf16)]
    keep = []
    for c, start in enumerate(starts):
        own = call(
            functools.partial(own_kernel, half, start),
            shaped((rows, size), f32),
            (act, down_near),
            8 * mib,
            cost=work,
        )
        total, sent = call(
            functools.partial(side_kernel, start), kept, (own, came[c], hidden_in), 8 * mib
        )
        keep.append(total)
        came[c] = swapped(sent, 2)
    bit = 4
    while bit < n:
        for c in range(CHUNKS):
            keep[c], sent = call(
                sum_kernel,
                kept,
                (keep[c], came[c]),
                8 * mib,
                cost=ahead(codes) if bit == 4 and c == 0 else None,
            )
            came[c] = swapped(sent, bit)
        bit *= 2
    route = call(
        functools.partial(route_kernel, lists_dev, capacity),
        shaped((n * capacity, LANES), jnp.int32),
        (probes, list_slot[None], counts[None], keep[-1]),
        4 * mib,
    )
    wanted = call(
        functools.partial(wanted_kernel, capacity, q_dev, PROBES),
        shaped((n * capacity, LANES), jnp.int32),
        (here, list_slot[None], route),
        4 * mib,
    )
    near = [
        call(
            functools.partial(scale_kernel, start),
            shaped((side_rows, size + LANES), bf16),
            (keep[c], came[c], final_gain[None], wanted),
            8 * mib,
        )
        for c, start in enumerate(starts)
    ]
    far = [swapped(x, 2) for x in near]
    near_other = [swapped(x, 1) for x in near]
    far_other = [swapped(x, 1) for x in far]
    scales_near = jnp.swapaxes(scales, 1, 2)
    scratch = [VMEM((n * capacity, size), bf16), VMEM((2 * n * capacity, size), bf16)]
    pieces = [(True, c, near[c], far[c]) for c in range(CHUNKS)]
    pieces += [(False, c, near_other[c], far_other[c]) for c in range(CHUNKS)]
    sofar = []
    for mine, c, here_rows, there_rows in pieces[:-1]:
        sofar = call(
            functools.partial(some_scores_kernel, mine, starts[c]),
            [shaped((n * capacity, list_rows), f32), shaped((n * capacity, LANES), f32)],
            (here_rows, there_rows, wanted, codes_near, scales_near, *sofar),
            8 * mib,
            cost=products(n * capacity * lists_dev * list_rows * size),
            scratch=scratch,
        )
    mine, c, here_rows, there_rows = pieces[-1]
    scores = call(
        functools.partial(last_scores_kernel, mine, starts[c]),
        shaped((n, capacity, list_rows), f32),
        (here_rows, there_rows, wanted, codes_near, scales_near, *sofar),
        8 * mib,
        scratch=scratch,
    )
    back = exchange(scores)
    return call(best_kernel, shaped((q_dev, K_TOP), f32), (back, route), 8 * mib)


def solution(mesh):
    in_specs = (
        P(("grp", "wide"), None),
        P(),
        P(None, "wide"),
        P(None, "wide"),
        P("wide", None),
        P(),
        P(("grp", "wide"), None, None),
        P(("grp", "wide"), None, None),
        P("grp"),
        P("grp"),
        P(("grp", "wide"), None),
    )
    out_specs = P(("grp", "wide"), None)
    return jax.shard_map(body, mesh=mesh, in_specs=in_specs, out_specs=out_specs, check_vma=False)
```

```python
import functools

import jax
import jax.numpy as jnp
from jax import lax
from jax.experimental import pallas as pl
from jax.experimental.pallas import tpu as pltpu
from jax.sharding import PartitionSpec as P


PROBES = 8
K_TOP = 8
BLOCK = 128
LANES = 128
DIGIT = 256
CHUNKS = 2


floor_score = -1e30

VMEM = pltpu.VMEM


def call(kernel, out_shape, args, vmem, cost=None, scratch=()):
    many = isinstance(out_shape, (list, tuple))
    return pl.pallas_call(
        kernel,
        out_shape=out_shape,
        in_specs=[pl.BlockSpec(memory_space=VMEM)] * len(args),
        out_specs=[pl.BlockSpec(memory_space=VMEM)] * len(out_shape)
        if many
        else pl.BlockSpec(memory_space=VMEM),
        scratch_shapes=list(scratch),
        compiler_params=pltpu.CompilerParams(vmem_limit_bytes=vmem),
        cost_estimate=cost,
    )(*args)


def ahead(*arrays):
    total = sum(a.size * a.dtype.itemsize for a in arrays)
    return pl.CostEstimate(flops=1000 * total, bytes_accessed=1 << 20, transcendentals=0)


def products(count):
    return pl.CostEstimate(flops=2 * count, bytes_accessed=1 << 20, transcendentals=0)


def shaped(shape, dtype):
    return jax.ShapeDtypeStruct(shape, dtype)


def norm_kernel(hidden_ref, gain_ref, probes_ref, out_ref, rows_ref, scale_ref, ids_ref, sems):
    copies = [
        pltpu.make_async_copy(source, target, sems.at[index])
        for index, (source, target) in enumerate(
            [(hidden_ref, rows_ref), (gain_ref, scale_ref), (probes_ref, ids_ref)]
        )
    ]
    for copy in copies:
        copy.start()
    for copy in copies:
        copy.wait()
    rows = rows_ref[...].astype(jnp.float32)
    width = rows.shape[1]
    scale = lax.rsqrt(jnp.mean(rows * rows, axis=-1, keepdims=True) + 1e-05)
    out_ref[:, :width] = (rows * scale * scale_ref[...]).astype(jnp.bfloat16)

    q_dev, probes = ids_ref.shape
    pairs = q_dev * probes
    lane = lax.broadcasted_iota(jnp.int32, (q_dev, LANES), 1)
    query = lax.broadcasted_iota(jnp.int32, (q_dev, LANES), 0)
    ids = jnp.zeros((q_dev, LANES), jnp.int32)
    for j in range(probes):
        ids = jnp.where(lane % probes == j, ids_ref[:, j : j + 1], ids)
    ids = jnp.where((lane % pairs) // probes == query, ids, 0)
    ids = jnp.sum(ids, axis=0, keepdims=True)
    digits = jnp.where(lane < pairs, ids // DIGIT, ids % DIGIT)
    digits = jnp.where(lane < 2 * pairs, digits, 0)
    out_ref[:, width:] = digits.astype(jnp.float32).astype(jnp.bfloat16)


def spread_kernel(normed_ref, out_ref):
    half = out_ref.shape[2] - LANES
    for k in range(out_ref.shape[0]):
        core = k % 2
        out_ref[k, :, :half] = normed_ref[:, core * half : (core + 1) * half]
        out_ref[k, :, half:] = normed_ref[:, 2 * half :]


def wanted_kernel(capacity, q_dev, probes, here_ref, slot_ref, after_ref, out_ref):
    devices, _, wide = here_ref.shape
    half = wide - LANES
    lists = slot_ref.shape[1]
    pairs = q_dev * probes
    lists_dev = lists // devices
    me = lax.axis_index("wide")
    tails = here_ref[:, :, half:].astype(jnp.float32)
    tails = jnp.max(tails, axis=1).astype(jnp.int32)
    ids = tails[:, :pairs] * DIGIT + tails[:, pairs : 2 * pairs]
    number = lax.broadcasted_iota(jnp.int32, (1, lists), 1)
    local = jnp.full((devices, pairs), -1, jnp.int32)
    for index in range(lists_dev):
        held = slot_ref[...] == me * lists_dev + index
        mine = jnp.sum(jnp.where(held, number, 0), axis=1, keepdims=True)
        local = jnp.where(ids == mine, index, local)
    pair = lax.broadcasted_iota(jnp.int32, (devices, pairs), 1)
    home = lax.broadcasted_iota(jnp.int32, (devices, 1), 0)
    place = lax.broadcasted_iota(jnp.int32, (devices, LANES), 1)
    side = lax.rem(me, 4) // 2
    before = jnp.full((devices, 1), -1, jnp.int32)
    for rank in range(capacity):
        open_pair = (local >= 0) & (pair > before)
        chosen = jnp.min(jnp.where(open_pair, pair, pairs), axis=1, keepdims=True)
        there = jnp.sum(jnp.where(pair == chosen, local, 0), axis=1, keepdims=True)
        row = jnp.where(
            lax.rem(home, 4) // 2 == side, 0, devices * q_dev // 2
        ) + home // 4 * (2 * q_dev) + lax.rem(home, 2) * q_dev + chosen // probes
        row = jnp.where(chosen < pairs, row, -1)
        out_ref[rank * devices : (rank + 1) * devices, :] = jnp.where(
            place == 0, row, jnp.where(place == 1, there, 0)
        )
        before = chosen


def route_kernel(lists_dev, capacity, probes_ref, slot_ref, count_ref, after_ref, out_ref):
    q_dev, probes = probes_ref.shape
    lists = slot_ref.shape[1]
    pairs = q_dev * probes
    slots = out_ref.shape[0]
    ids = jnp.concatenate(
        [jnp.broadcast_to(probes_ref[q : q + 1, :], (probes, probes)) for q in range(q_dev)], axis=0
    )
    sub = lax.broadcasted_iota(jnp.int32, (pairs, probes), 0)
    lane = lax.broadcasted_iota(jnp.int32, (pairs, probes), 1)
    ids = jnp.sum(jnp.where(sub % probes == lane, ids, 0), axis=1, keepdims=True)
    hit = lax.broadcasted_iota(jnp.int32, (pairs, lists), 1) == ids
    slot = jnp.sum(jnp.where(hit, slot_ref[...], 0), axis=1, keepdims=True)
    valid = jnp.sum(jnp.where(hit, count_ref[...], 0), axis=1, keepdims=True)
    owner = slot // lists_dev
    local = slot % lists_dev
    p_sub = lax.broadcasted_iota(jnp.int32, (pairs, pairs), 0)
    p_lane = lax.broadcasted_iota(jnp.int32, (pairs, pairs), 1)
    diagonal = p_sub == p_lane

    def as_row(column):
        return jnp.sum(jnp.where(diagonal, column, 0), axis=0, keepdims=True)

    owner_row = as_row(owner)
    rank_row = jnp.sum(
        jnp.where((owner == owner_row) & (p_sub < p_lane), 1, 0), axis=0, keepdims=True
    )
    target_row = owner_row * capacity + rank_row
    here = lax.broadcasted_iota(jnp.int32, (slots, pairs), 0) == target_row
    pair_row = lax.broadcasted_iota(jnp.int32, (slots, pairs), 1)

    def of_slot(row):
        return jnp.sum(jnp.where(here, row, 0), axis=1, keepdims=True)

    query = of_slot(pair_row // probes + 1) - 1
    place = lax.broadcasted_iota(jnp.int32, (slots, LANES), 1)
    out = jnp.where(place == 0, query, 0)
    out = jnp.where(place == 1, of_slot(as_row(local)), out)
    out_ref[...] = jnp.where(place == 2, of_slot(as_row(valid)), out)


def my_span(mine, half, start, size):
    core = lax.rem(lax.axis_index("wide"), 2)
    which = core if mine else 1 - core
    return pl.ds(pl.multiple_of(which * half + start, size), size)


def first_kernel(here_ref, gate_ref, up_ref, after_ref, gate_out, up_out, rows_ref):
    rows_ref[...] = here_ref[:, :, : rows_ref.shape[1]].reshape(rows_ref.shape)
    half = rows_ref.shape[1]
    span = my_span(True, half, 0, half)
    gate_out[...] = jnp.dot(rows_ref[...], gate_ref[span, :], preferred_element_type=jnp.float32)
    up_out[...] = jnp.dot(rows_ref[...], up_ref[span, :], preferred_element_type=jnp.float32)


def put_share(act_ref, down_ref, hidden_ref, send_ref, half, start):
    rows, size = act_ref.shape[0], send_ref.shape[1]
    span = my_span(False, half, start, size)
    send_ref[:rows, :] = jnp.dot(
        act_ref[...], down_ref[:, span], preferred_element_type=jnp.float32
    ).astype(jnp.bfloat16)
    residual = hidden_ref[:, span]
    send_ref[rows:, :] = jnp.concatenate([residual, residual], axis=0)


def second_kernel(
    there_ref, gate_part, up_part, gate_ref, up_ref, down_ref, hidden_ref, act_ref, send_ref, rows_ref
):
    half = rows_ref.shape[1]
    rows_ref[...] = there_ref[:, :, :half].reshape(rows_ref.shape)
    span = my_span(False, half, 0, half)
    gate = gate_part[...] + jnp.dot(
        rows_ref[...], gate_ref[span, :], preferred_element_type=jnp.float32
    )
    up = up_part[...] + jnp.dot(
        rows_ref[...], up_ref[span, :], preferred_element_type=jnp.float32
    )
    act_ref[...] = (gate / (1.0 + jnp.exp(-gate)) * up).astype(jnp.bfloat16)
    put_share(act_ref, down_ref, hidden_ref, send_ref, half, 0)


def share_kernel(half, start, act_ref, down_ref, hidden_ref, send_ref):
    put_share(act_ref, down_ref, hidden_ref, send_ref, half, start)


def own_kernel(half, start, act_ref, down_ref, own_ref):
    span = my_span(True, half, start, own_ref.shape[1])
    own_ref[...] = jnp.dot(act_ref[...], down_ref[:, span], preferred_element_type=jnp.float32)


def side_kernel(start, own_ref, came_ref, hidden_ref, keep_ref, send_ref):
    rows, size = own_ref.shape
    q_dev, width = hidden_ref.shape
    half = width // 2
    me = lax.axis_index("wide")
    core, side, plane = lax.rem(me, 2), lax.rem(me, 4) // 2, me // 4
    group = 2 * q_dev
    mine = jnp.where(
        core == 0,
        hidden_ref[:, start : start + size],
        hidden_ref[:, half + start : half + start + size],
    ).astype(jnp.float32)
    other = came_ref[rows : rows + q_dev, :].astype(jnp.float32)
    residual = jnp.where(
        core == 0,
        jnp.concatenate([mine, other], axis=0),
        jnp.concatenate([other, mine], axis=0),
    )
    for z in range(rows // (2 * group)):
        total = []
        for y in range(2):
            span = slice((2 * z + y) * group, (2 * z + y + 1) * group)
            total.append(own_ref[span, :] + came_ref[span, :].astype(jnp.float32))
        kept = jnp.where(side == 0, total[0], total[1])
        sent = jnp.where(side == 0, total[1], total[0])
        span = slice(z * group, (z + 1) * group)
        keep_ref[span, :] = kept + jnp.where(plane == z, residual, jnp.zeros_like(residual))
        send_ref[span, :] = sent.astype(jnp.bfloat16)


def sum_kernel(keep_ref, came_ref, total_ref, send_ref):
    total = keep_ref[...] + came_ref[...].astype(jnp.float32)
    total_ref[...] = total
    send_ref[...] = total.astype(jnp.bfloat16)


def scale_kernel(start, keep_ref, came_ref, gain_ref, after_ref, out_ref):
    rows, size = keep_ref.shape
    half = gain_ref.shape[1] // 2
    core = lax.rem(lax.axis_index("wide"), 2)
    gain = jnp.where(
        core == 0,
        gain_ref[:, start : start + size],
        gain_ref[:, half + start : half + start + size],
    )
    scaled = gain * (keep_ref[...] + came_ref[...].astype(jnp.float32))
    out_ref[:, :size] = scaled.astype(jnp.bfloat16)
    left = jnp.sum(scaled * scaled, axis=-1, keepdims=True)
    lane = lax.broadcasted_iota(jnp.int32, (rows, LANES), 1)
    tail = jnp.zeros((rows, LANES), jnp.float32)
    for piece in range(3):
        part = left.astype(jnp.bfloat16).astype(jnp.float32)
        tail = jnp.where(lane == piece, part, tail)
        left = left - part
    out_ref[:, size:] = tail.astype(jnp.bfloat16)


def chunk_scores(
    mine, start, near_ref, far_ref, wanted_ref, codes_ref, scales_ref, picks_ref, rows_ref
):
    side_rows, wide = near_ref.shape
    size = wide - LANES
    lists, list_rows, width = codes_ref.shape
    half = width // 2
    pairs = wanted_ref.shape[0]
    row = wanted_ref[:, 0:1]
    local = wanted_ref[:, 1:2]
    column = lax.broadcasted_iota(jnp.int32, (pairs, side_rows), 1)

    def pick(ref, first):
        hot = jnp.where(column + first == row, 1.0, 0.0).astype(jnp.bfloat16)
        return jnp.dot(hot, ref[...], preferred_element_type=jnp.float32)

    chosen = pick(near_ref, 0) + pick(far_ref, side_rows)
    picks_ref[...] = chosen[:, :size].astype(jnp.bfloat16)
    nothing = jnp.zeros((pairs, BLOCK), jnp.bfloat16)
    for block in range(size // BLOCK):
        span = slice(block * BLOCK, (block + 1) * BLOCK)
        kept = block % 2
        rows_ref[kept * pairs : (kept + 1) * pairs, span] = picks_ref[:, span]
        rows_ref[(1 - kept) * pairs : (2 - kept) * pairs, span] = nothing
    squares = jnp.sum(chosen[:, size:], axis=1, keepdims=True)

    core = lax.rem(lax.axis_index("wide"), 2)
    which = core if mine else 1 - core
    blocks = size // BLOCK
    here = pl.ds(
        pl.multiple_of(which * (half // BLOCK) + start // BLOCK, blocks), blocks
    )
    picked = jnp.zeros((pairs, list_rows), jnp.float32)
    for first in range(0, lists, 2):
        scale = jnp.concatenate([scales_ref[first, here, :], scales_ref[first + 1, here, :]], axis=1)
        total = jnp.zeros((pairs, 2 * list_rows), jnp.float32)
        for step in range(blocks // 2):
            span = slice(step * 2 * BLOCK, (step + 1) * 2 * BLOCK)
            away = my_span(mine, half, start + step * 2 * BLOCK, 2 * BLOCK)
            part = lax.dot_general(
                rows_ref[:, span],
                codes_ref[first : first + 2, :, away].reshape(2 * list_rows, 2 * BLOCK),
                (((1,), (1,)), ((), ())),
                preferred_element_type=jnp.float32,
            )
            total += part[:pairs] * scale[2 * step : 2 * step + 1, :]
            total += part[pairs:] * scale[2 * step + 1 : 2 * step + 2, :]
        picked = jnp.where(local == first, total[:, :list_rows], picked)
        picked = jnp.where(local == first + 1, total[:, list_rows:], picked)
    return picked, squares


def some_scores_kernel(
    mine, start, near_ref, far_ref, wanted_ref, codes_ref, scales_ref, *rest
):
    *sofar, picked_ref, squares_ref, picks_ref, rows_ref = rest
    picked, squares = chunk_scores(
        mine, start, near_ref, far_ref, wanted_ref, codes_ref, scales_ref, picks_ref, rows_ref
    )
    if sofar:
        picked += sofar[0][...]
        squares = squares + sofar[1][...]
    picked_ref[...] = picked
    squares_ref[...] = jnp.broadcast_to(squares, squares_ref.shape)


def last_scores_kernel(mine, starts, *refs):
    chunks = len(starts)
    tables = refs[2 * chunks : 2 * chunks + 3]
    sofar_ref, squares_ref, out_ref, picks_ref, rows_ref = refs[2 * chunks + 3 :]
    scores, squares = sofar_ref[...], squares_ref[:, 0:1]
    for c, start in enumerate(starts):
        picked, more = chunk_scores(
            mine, start, refs[2 * c], refs[2 * c + 1], *tables, picks_ref.at[c], rows_ref.at[c]
        )
        scores += picked
        squares = squares + more
    scores = scores * lax.rsqrt(squares + 1e-06)
    devices, capacity, _ = out_ref.shape
    for rank in range(capacity):
        out_ref[:, rank, :] = scores[rank * devices : (rank + 1) * devices]


def best_kernel(back_ref, route_ref, out_ref):
    q_dev, count = out_ref.shape
    sources, slots, list_rows = back_ref.shape
    pairs = sources * slots
    scores = back_ref[...].reshape(pairs, list_rows)
    query = route_ref[:, 0:1]
    alive = lax.broadcasted_iota(jnp.int32, (pairs, list_rows), 1) < route_ref[:, 2:3]
    left = jnp.concatenate(
        [jnp.where(alive & (query == q), scores, floor_score)[None] for q in range(q_dev)], axis=0
    )
    column = lax.broadcasted_iota(jnp.int32, (q_dev, count), 1)
    best = jnp.zeros((q_dev, count), jnp.float32)
    filled = jnp.zeros((q_dev, 1), jnp.float32)
    for rank in range(count):
        top = jnp.max(jnp.max(left, axis=1), axis=-1, keepdims=True)
        best = jnp.where(column >= filled.astype(jnp.int32), top, best)
        if rank + 1 < count:
            same = left == top[:, :, None]
            filled += jnp.sum(
                jnp.sum(jnp.where(same, 1.0, 0.0), axis=1), axis=-1, keepdims=True
            )
            left = jnp.where(same, floor_score * 2, left)
    out_ref[...] = best


def body(
    hidden_in,
    ffn_gain,
    gate_weight,
    up_weight,
    down_weight,
    final_gain,
    codes,
    scales,
    counts,
    list_slot,
    probes,
):
    q_dev, width = hidden_in.shape
    hidden_units = gate_weight.shape[1]
    n = lax.axis_size("wide")
    half = width // 2
    rows = n * q_dev
    lists_dev, list_rows, _ = codes.shape
    capacity = (q_dev * PROBES + n - 1) // n
    mib = 1 << 20
    f32, bf16 = jnp.float32, jnp.bfloat16

    def exchange(x):
        return lax.all_to_all(x, "wide", 0, 0, tiled=True)

    def swapped(x, bit):
        return lax.ppermute(x, "wide", [(i, i ^ bit) for i in range(n)])

    gate_near = pltpu.with_memory_space_constraint(gate_weight, VMEM)
    up_near = pltpu.with_memory_space_constraint(up_weight, VMEM)
    down_near = pltpu.with_memory_space_constraint(down_weight, VMEM)
    codes_near = pltpu.with_memory_space_constraint(codes, VMEM)

    normed = pl.pallas_call(
        norm_kernel,
        out_shape=shaped((q_dev, width + LANES), bf16),
        in_specs=[pl.BlockSpec(memory_space=pltpu.HBM)] * 3,
        out_specs=pl.BlockSpec(memory_space=VMEM),
        scratch_shapes=[
            VMEM((q_dev, width), bf16),
            VMEM((1, width), f32),
            VMEM(probes.shape, jnp.int32),
            pltpu.SemaphoreType.DMA((3,)),
        ],
        compiler_params=pltpu.CompilerParams(vmem_limit_bytes=8 * mib),
    )(
        pltpu.with_memory_space_constraint(hidden_in, pltpu.HBM),
        pltpu.with_memory_space_constraint(ffn_gain[None], pltpu.HBM),
        pltpu.with_memory_space_constraint(probes, pltpu.HBM),
    )
    spread = call(
        spread_kernel,
        shaped((n, q_dev, half + LANES), bf16),
        (normed,),
        8 * mib,
        cost=ahead(gate_weight, up_weight, down_weight),
    )
    here = exchange(spread)
    there = swapped(here, 1)
    gate_part, up_part = call(
        first_kernel,
        [shaped((rows, hidden_units), f32)] * 2,
        (here, gate_near, up_near, down_near),
        8 * mib,
        cost=products(rows * half * hidden_units * 2),
        scratch=[VMEM((rows, half), bf16)],
    )
    size = half // CHUNKS
    starts = [c * size for c in range(CHUNKS)]
    share = shaped((rows + 2 * q_dev, size), bf16)
    act, sent = call(
        second_kernel,
        [shaped((rows, hidden_units), bf16), share],
        (there, gate_part, up_part, gate_near, up_near, down_near, hidden_in),
        8 * mib,
        scratch=[VMEM((rows, half), bf16)],
    )
    came = [swapped(sent, 1)]
    work = products(rows * size * hidden_units)
    for start in starts[1:]:
        sent = call(
            functools.partial(share_kernel, half, start),
            share,
            (act, down_near, hidden_in),
            8 * mib,
            cost=work,
        )
        came.append(swapped(sent, 1))
    side_rows = rows // 2
    kept = [shaped((side_rows, size), f32), shaped((side_rows, size), bf16)]
    keep = []
    for c, start in enumerate(starts):
        own = call(
            functools.partial(own_kernel, half, start),
            shaped((rows, size), f32),
            (act, down_near),
            8 * mib,
            cost=work,
        )
        total, sent = call(
            functools.partial(side_kernel, start), kept, (own, came[c], hidden_in), 8 * mib
        )
        keep.append(total)
        came[c] = swapped(sent, 2)
    bit = 4
    while bit < n:
        for c in range(CHUNKS):
            keep[c], sent = call(
                sum_kernel,
                kept,
                (keep[c], came[c]),
                8 * mib,
                cost=ahead(codes) if bit == 4 and c == 0 else None,
            )
            came[c] = swapped(sent, bit)
        bit *= 2
    route = call(
        functools.partial(route_kernel, lists_dev, capacity),
        shaped((n * capacity, LANES), jnp.int32),
        (probes, list_slot[None], counts[None], keep[-1]),
        4 * mib,
    )
    wanted = call(
        functools.partial(wanted_kernel, capacity, q_dev, PROBES),
        shaped((n * capacity, LANES), jnp.int32),
        (here, list_slot[None], route),
        4 * mib,
    )
    near = [
        call(
            functools.partial(scale_kernel, start),
            shaped((side_rows, size + LANES), bf16),
            (keep[c], came[c], final_gain[None], wanted),
            8 * mib,
        )
        for c, start in enumerate(starts)
    ]
    far = []
    for x in near:
        far.append(swapped(x, 2))
    near_other = [swapped(x, 1) for x in near]
    far_other = [swapped(x, 1) for x in far]
    scales_near = jnp.swapaxes(scales, 1, 2)
    pairs = n * capacity
    sofar = []
    for c, start in enumerate(starts):
        sofar = call(
            functools.partial(some_scores_kernel, True, start),
            [shaped((pairs, list_rows), f32), shaped((pairs, LANES), f32)],
            (near[c], far[c], wanted, codes_near, scales_near, *sofar),
            8 * mib,
            cost=products(pairs * lists_dev * list_rows * size),
            scratch=[VMEM((pairs, size), bf16), VMEM((2 * pairs, size), bf16)],
        )
    others = [x for pair in zip(near_other, far_other) for x in pair]
    scores = call(
        functools.partial(last_scores_kernel, False, starts),
        shaped((n, capacity, list_rows), f32),
        (*others, wanted, codes_near, scales_near, *sofar),
        8 * mib,
        scratch=[VMEM((CHUNKS, pairs, size), bf16), VMEM((CHUNKS, 2 * pairs, size), bf16)],
    )
    back = exchange(scores)
    return call(best_kernel, shaped((q_dev, K_TOP), f32), (back, route), 8 * mib)


def solution(mesh):
    in_specs = (
        P(("grp", "wide"), None),
        P(),
        P(None, "wide"),
        P(None, "wide"),
        P("wide", None),
        P(),
        P(("grp", "wide"), None, None),
        P(("grp", "wide"), None, None),
        P("grp"),
        P("grp"),
        P(("grp", "wide"), None),
    )
    out_specs = P(("grp", "wide"), None)
    return jax.shard_map(body, mesh=mesh, in_specs=in_specs, out_specs=out_specs, check_vma=False)
```

```python
import functools

import jax
import jax.numpy as jnp
from jax import lax
from jax.experimental import pallas as pl
from jax.experimental.pallas import tpu as pltpu
from jax.sharding import PartitionSpec as P


PROBES = 8
K_TOP = 8
BLOCK = 128
LANES = 128
DIGIT = 256
CHUNKS = 2


floor_score = -1e30

VMEM = pltpu.VMEM


def call(kernel, out_shape, args, vmem, cost=None, scratch=()):
    many = isinstance(out_shape, (list, tuple))
    return pl.pallas_call(
        kernel,
        out_shape=out_shape,
        in_specs=[pl.BlockSpec(memory_space=VMEM)] * len(args),
        out_specs=[pl.BlockSpec(memory_space=VMEM)] * len(out_shape)
        if many
        else pl.BlockSpec(memory_space=VMEM),
        scratch_shapes=list(scratch),
        compiler_params=pltpu.CompilerParams(vmem_limit_bytes=vmem),
        cost_estimate=cost,
    )(*args)


def ahead(*arrays):
    total = sum(a.size * a.dtype.itemsize for a in arrays)
    return pl.CostEstimate(flops=1000 * total, bytes_accessed=1 << 20, transcendentals=0)


def products(count):
    return pl.CostEstimate(flops=2 * count, bytes_accessed=1 << 20, transcendentals=0)


def shaped(shape, dtype):
    return jax.ShapeDtypeStruct(shape, dtype)


def by_core(own, other):
    core = lax.rem(lax.axis_index("wide"), 2)
    return jnp.where(
        core == 0,
        jnp.concatenate([own, other], axis=0),
        jnp.concatenate([other, own], axis=0),
    )


def half_of(ref, start, size):
    half = ref.shape[1] // 2
    core = lax.rem(lax.axis_index("wide"), 2)
    return jnp.where(
        core == 0, ref[:, start : start + size], ref[:, half + start : half + start + size]
    )


def norm_rows(rows, gain):
    scale = lax.rsqrt(jnp.mean(rows * rows, axis=-1, keepdims=True) + 1e-05)
    return (rows * scale * gain).astype(jnp.bfloat16)


def digits_of(ids_ref):
    q_dev, probes = ids_ref.shape
    pairs = q_dev * probes
    lane = lax.broadcasted_iota(jnp.int32, (q_dev, LANES), 1)
    query = lax.broadcasted_iota(jnp.int32, (q_dev, LANES), 0)
    ids = jnp.zeros((q_dev, LANES), jnp.int32)
    for j in range(probes):
        ids = jnp.where(lane % probes == j, ids_ref[:, j : j + 1], ids)
    ids = jnp.where((lane % pairs) // probes == query, ids, 0)
    ids = jnp.sum(ids, axis=0, keepdims=True)
    digit = jnp.where(lane < pairs, ids // DIGIT, ids % DIGIT)
    return jnp.where(lane < 2 * pairs, digit, 0).astype(jnp.float32).astype(jnp.bfloat16)


def norm_kernel(hidden_ref, gain_ref, probes_ref, out_ref, rows_ref, scale_ref, ids_ref, sems):
    copies = [
        pltpu.make_async_copy(source, target, sems.at[index])
        for index, (source, target) in enumerate(
            [(hidden_ref, rows_ref), (gain_ref, scale_ref), (probes_ref, ids_ref)]
        )
    ]
    for copy in copies:
        copy.start()
    for copy in copies:
        copy.wait()
    width = rows_ref.shape[1]
    out_ref[:, :width] = norm_rows(rows_ref[...].astype(jnp.float32), scale_ref[...])
    out_ref[:, width:] = digits_of(ids_ref)


def chip_kernel(
    normed_ref, rows_ref, scale_ref, hidden_other, probes_other, out_ref, residual_ref
):
    half = out_ref.shape[1] - LANES
    width = 2 * half
    other = hidden_other[...].astype(jnp.float32)
    residual_ref[...] = by_core(rows_ref[...].astype(jnp.float32), other).astype(jnp.bfloat16)
    other = norm_rows(other, scale_ref[...]).astype(jnp.float32)
    normed = by_core(normed_ref[:, :width].astype(jnp.float32), other)
    core = lax.rem(lax.axis_index("wide"), 2)
    out_ref[:, :half] = jnp.where(core == 0, normed[:, :half], normed[:, half:]).astype(
        jnp.bfloat16
    )
    tails = by_core(
        normed_ref[:, width:].astype(jnp.float32), digits_of(probes_other).astype(jnp.float32)
    )
    out_ref[:, half:] = tails.astype(jnp.bfloat16)


def join_kernel(here_ref, came_ref, out_ref):
    rows = here_ref.shape[0]
    out_ref[:rows, :] = here_ref[...]
    out_ref[rows:, :] = came_ref[...]


def wanted_kernel(
    capacity, q_dev, probes, devices, places, near_ref, far_ref, slot_ref, after_ref, out_ref
):
    side_rows, wide = near_ref.shape
    half = wide - LANES
    lists = slot_ref.shape[1]
    pairs = q_dev * probes
    lists_dev = lists // devices
    me = lax.axis_index("wide")
    home = lax.broadcasted_iota(jnp.int32, (devices, 1), 0)
    apart = jnp.bitwise_xor(home // 2, me // 2)
    first = apart % 2 * side_rows + home % 2 * q_dev
    for bit, move in places:
        first = first + apart // (bit // 2) % 2 * move
    column = lax.broadcasted_iota(jnp.int32, (devices, side_rows), 1)

    def tails(ref, start):
        hot = jnp.where(column + start == first, 1.0, 0.0).astype(jnp.bfloat16)
        return jnp.dot(hot, ref[:, half:], preferred_element_type=jnp.float32)

    digits = (tails(near_ref, 0) + tails(far_ref, side_rows)).astype(jnp.int32)
    ids = digits[:, :pairs] * DIGIT + digits[:, pairs : 2 * pairs]
    number = lax.broadcasted_iota(jnp.int32, (1, lists), 1)
    local = jnp.full((devices, pairs), -1, jnp.int32)
    for index in range(lists_dev):
        held = slot_ref[...] == me * lists_dev + index
        mine = jnp.sum(jnp.where(held, number, 0), axis=1, keepdims=True)
        local = jnp.where(ids == mine, index, local)
    pair = lax.broadcasted_iota(jnp.int32, (devices, pairs), 1)
    place = lax.broadcasted_iota(jnp.int32, (devices, LANES), 1)
    before = jnp.full((devices, 1), -1, jnp.int32)
    for rank in range(capacity):
        open_pair = (local >= 0) & (pair > before)
        chosen = jnp.min(jnp.where(open_pair, pair, pairs), axis=1, keepdims=True)
        there = jnp.sum(jnp.where(pair == chosen, local, 0), axis=1, keepdims=True)
        row = jnp.where(chosen < pairs, first + chosen // probes, -1)
        out_ref[rank * devices : (rank + 1) * devices, :] = jnp.where(
            place == 0, row, jnp.where(place == 1, there, 0)
        )
        before = chosen


def route_kernel(lists_dev, capacity, probes_ref, slot_ref, count_ref, after_ref, out_ref):
    q_dev, probes = probes_ref.shape
    lists = slot_ref.shape[1]
    pairs = q_dev * probes
    slots = out_ref.shape[0]
    ids = jnp.concatenate(
        [jnp.broadcast_to(probes_ref[q : q + 1, :], (probes, probes)) for q in range(q_dev)], axis=0
    )
    sub = lax.broadcasted_iota(jnp.int32, (pairs, probes), 0)
    lane = lax.broadcasted_iota(jnp.int32, (pairs, probes), 1)
    ids = jnp.sum(jnp.where(sub % probes == lane, ids, 0), axis=1, keepdims=True)
    hit = lax.broadcasted_iota(jnp.int32, (pairs, lists), 1) == ids
    slot = jnp.sum(jnp.where(hit, slot_ref[...], 0), axis=1, keepdims=True)
    valid = jnp.sum(jnp.where(hit, count_ref[...], 0), axis=1, keepdims=True)
    owner = slot // lists_dev
    local = slot % lists_dev
    p_sub = lax.broadcasted_iota(jnp.int32, (pairs, pairs), 0)
    p_lane = lax.broadcasted_iota(jnp.int32, (pairs, pairs), 1)
    diagonal = p_sub == p_lane

    def as_row(column):
        return jnp.sum(jnp.where(diagonal, column, 0), axis=0, keepdims=True)

    owner_row = as_row(owner)
    rank_row = jnp.sum(
        jnp.where((owner == owner_row) & (p_sub < p_lane), 1, 0), axis=0, keepdims=True
    )
    target_row = owner_row * capacity + rank_row
    here = lax.broadcasted_iota(jnp.int32, (slots, pairs), 0) == target_row
    pair_row = lax.broadcasted_iota(jnp.int32, (slots, pairs), 1)

    def of_slot(row):
        return jnp.sum(jnp.where(here, row, 0), axis=1, keepdims=True)

    query = of_slot(pair_row // probes + 1) - 1
    place = lax.broadcasted_iota(jnp.int32, (slots, LANES), 1)
    out = jnp.where(place == 0, query, 0)
    out = jnp.where(place == 1, of_slot(as_row(local)), out)
    out_ref[...] = jnp.where(place == 2, of_slot(as_row(valid)), out)


def my_span(mine, half, start, size):
    core = lax.rem(lax.axis_index("wide"), 2)
    which = core if mine else 1 - core
    return pl.ds(pl.multiple_of(which * half + start, size), size)


def fill_rows(rows_ref, near_ref, far_ref):
    half = rows_ref.shape[1]
    side_rows = near_ref.shape[0]
    rows_ref[:side_rows, :] = near_ref[:, :half]
    rows_ref[side_rows:, :] = far_ref[:, :half]


def first_kernel(near_ref, far_ref, gate_ref, up_ref, after_ref, gate_out, up_out, rows_ref):
    fill_rows(rows_ref, near_ref, far_ref)
    half = rows_ref.shape[1]
    span = my_span(True, half, 0, half)
    gate_out[...] = jnp.dot(rows_ref[...], gate_ref[span, :], preferred_element_type=jnp.float32)
    up_out[...] = jnp.dot(rows_ref[...], up_ref[span, :], preferred_element_type=jnp.float32)


def share_kernel(half, start, act_ref, down_ref, send_ref):
    span = my_span(False, half, start, send_ref.shape[1])
    send_ref[...] = jnp.dot(
        act_ref[...], down_ref[:, span], preferred_element_type=jnp.float32
    ).astype(jnp.bfloat16)


def second_kernel(
    near_ref, far_ref, gate_part, up_part, gate_ref, up_ref, down_ref, act_ref, send_ref, rows_ref
):
    fill_rows(rows_ref, near_ref, far_ref)
    half = rows_ref.shape[1]
    span = my_span(False, half, 0, half)
    gate = gate_part[...] + jnp.dot(
        rows_ref[...], gate_ref[span, :], preferred_element_type=jnp.float32
    )
    up = up_part[...] + jnp.dot(
        rows_ref[...], up_ref[span, :], preferred_element_type=jnp.float32
    )
    act_ref[...] = (gate / (1.0 + jnp.exp(-gate)) * up).astype(jnp.bfloat16)
    share_kernel(half, 0, act_ref, down_ref, send_ref)


def own_kernel(half, start, act_ref, down_ref, own_ref):
    span = my_span(True, half, start, own_ref.shape[1])
    own_ref[...] = jnp.dot(act_ref[...], down_ref[:, span], preferred_element_type=jnp.float32)


def side_kernel(start, own_ref, came_ref, residual_ref, keep_ref, send_ref):
    side_rows, size = keep_ref.shape
    chip_rows = residual_ref.shape[0]
    total = own_ref[:side_rows, :] + came_ref[:side_rows, :].astype(jnp.float32)
    residual = half_of(residual_ref, start, size).astype(jnp.float32)
    keep_ref[:chip_rows, :] = total[:chip_rows] + residual
    keep_ref[chip_rows:, :] = total[chip_rows:]
    sent = own_ref[side_rows:, :] + came_ref[side_rows:, :].astype(jnp.float32)
    send_ref[...] = sent.astype(jnp.bfloat16)


def met(came_ref, move):
    rows = came_ref.shape[0]
    blocks = [came_ref[start : start + move, :] for start in range(0, rows, move)]
    turned = [blocks[index ^ 1] for index in range(len(blocks))]
    return jnp.concatenate([block.astype(jnp.float32) for block in turned], axis=0)


def sum_kernel(move, keep_ref, came_ref, total_ref, send_ref):
    came = met(came_ref, move) if move else came_ref[...].astype(jnp.float32)
    total = keep_ref[...] + came
    total_ref[...] = total
    send_ref[...] = total.astype(jnp.bfloat16)


def scale_kernel(start, move, keep_ref, came_ref, gain_ref, after_ref, out_ref):
    rows, size = keep_ref.shape
    gain = half_of(gain_ref, start, size)
    came = met(came_ref, move) if move else came_ref[...].astype(jnp.float32)
    scaled = gain * (keep_ref[...] + came)
    out_ref[:, :size] = scaled.astype(jnp.bfloat16)
    left = jnp.sum(scaled * scaled, axis=-1, keepdims=True)
    lane = lax.broadcasted_iota(jnp.int32, (rows, LANES), 1)
    tail = jnp.zeros((rows, LANES), jnp.float32)
    for piece in range(3):
        part = left.astype(jnp.bfloat16).astype(jnp.float32)
        tail = jnp.where(lane == piece, part, tail)
        left = left - part
    out_ref[:, size:] = tail.astype(jnp.bfloat16)


def chunk_scores(
    mine, start, near_ref, far_ref, wanted_ref, codes_ref, scales_ref, picks_ref, rows_ref
):
    side_rows, wide = near_ref.shape
    size = wide - LANES
    lists, list_rows, width = codes_ref.shape
    half = width // 2
    pairs = wanted_ref.shape[0]
    row = wanted_ref[:, 0:1]
    local = wanted_ref[:, 1:2]
    column = lax.broadcasted_iota(jnp.int32, (pairs, side_rows), 1)

    def pick(ref, first):
        hot = jnp.where(column + first == row, 1.0, 0.0).astype(jnp.bfloat16)
        return jnp.dot(hot, ref[...], preferred_element_type=jnp.float32)

    chosen = pick(near_ref, 0) + pick(far_ref, side_rows)
    picks_ref[...] = chosen[:, :size].astype(jnp.bfloat16)
    nothing = jnp.zeros((pairs, BLOCK), jnp.bfloat16)
    for block in range(size // BLOCK):
        span = slice(block * BLOCK, (block + 1) * BLOCK)
        kept = block % 2
        rows_ref[kept * pairs : (kept + 1) * pairs, span] = picks_ref[:, span]
        rows_ref[(1 - kept) * pairs : (2 - kept) * pairs, span] = nothing
    squares = jnp.sum(chosen[:, size:], axis=1, keepdims=True)

    core = lax.rem(lax.axis_index("wide"), 2)
    which = core if mine else 1 - core
    blocks = size // BLOCK
    here = pl.ds(
        pl.multiple_of(which * (half // BLOCK) + start // BLOCK, blocks), blocks
    )
    picked = jnp.zeros((pairs, list_rows), jnp.float32)
    for first in range(0, lists, 2):
        scale = jnp.concatenate([scales_ref[first, here, :], scales_ref[first + 1, here, :]], axis=1)
        total = jnp.zeros((pairs, 2 * list_rows), jnp.float32)
        for step in range(blocks // 2):
            span = slice(step * 2 * BLOCK, (step + 1) * 2 * BLOCK)
            away = my_span(mine, half, start + step * 2 * BLOCK, 2 * BLOCK)
            part = lax.dot_general(
                rows_ref[:, span],
                codes_ref[first : first + 2, :, away].reshape(2 * list_rows, 2 * BLOCK),
                (((1,), (1,)), ((), ())),
                preferred_element_type=jnp.float32,
            )
            total += part[:pairs] * scale[2 * step : 2 * step + 1, :]
            total += part[pairs:] * scale[2 * step + 1 : 2 * step + 2, :]
        picked = jnp.where(local == first, total[:, :list_rows], picked)
        picked = jnp.where(local == first + 1, total[:, list_rows:], picked)
    return picked, squares


def some_scores_kernel(
    mine, start, near_ref, far_ref, wanted_ref, codes_ref, scales_ref, *rest
):
    *sofar, picked_ref, squares_ref, picks_ref, rows_ref = rest
    picked, squares = chunk_scores(
        mine, start, near_ref, far_ref, wanted_ref, codes_ref, scales_ref, picks_ref, rows_ref
    )
    if sofar:
        picked += sofar[0][...]
        squares = squares + sofar[1][...]
    picked_ref[...] = picked
    squares_ref[...] = jnp.broadcast_to(squares, squares_ref.shape)


def last_scores_kernel(mine, starts, *refs):
    chunks = len(starts)
    tables = refs[2 * chunks : 2 * chunks + 3]
    sofar_ref, squares_ref, out_ref, picks_ref, rows_ref = refs[2 * chunks + 3 :]
    scores, squares = sofar_ref[...], squares_ref[:, 0:1]
    for c, start in enumerate(starts):
        picked, more = chunk_scores(
            mine, start, refs[2 * c], refs[2 * c + 1], *tables, picks_ref.at[c], rows_ref.at[c]
        )
        scores += picked
        squares = squares + more
    scores = scores * lax.rsqrt(squares + 1e-06)
    devices, capacity, _ = out_ref.shape
    for rank in range(capacity):
        out_ref[:, rank, :] = scores[rank * devices : (rank + 1) * devices]


def best_kernel(back_ref, route_ref, out_ref):
    q_dev, count = out_ref.shape
    sources, slots, list_rows = back_ref.shape
    pairs = sources * slots
    scores = back_ref[...].reshape(pairs, list_rows)
    query = route_ref[:, 0:1]
    alive = lax.broadcasted_iota(jnp.int32, (pairs, list_rows), 1) < route_ref[:, 2:3]
    left = jnp.concatenate(
        [jnp.where(alive & (query == q), scores, floor_score)[None] for q in range(q_dev)], axis=0
    )
    column = lax.broadcasted_iota(jnp.int32, (q_dev, count), 1)
    best = jnp.zeros((q_dev, count), jnp.float32)
    filled = jnp.zeros((q_dev, 1), jnp.float32)
    for rank in range(count):
        top = jnp.max(jnp.max(left, axis=1), axis=-1, keepdims=True)
        best = jnp.where(column >= filled.astype(jnp.int32), top, best)
        if rank + 1 < count:
            same = left == top[:, :, None]
            filled += jnp.sum(
                jnp.sum(jnp.where(same, 1.0, 0.0), axis=1), axis=-1, keepdims=True
            )
            left = jnp.where(same, floor_score * 2, left)
    out_ref[...] = best


def body(
    hidden_in,
    ffn_gain,
    gate_weight,
    up_weight,
    down_weight,
    final_gain,
    codes,
    scales,
    counts,
    list_slot,
    probes,
):
    q_dev, width = hidden_in.shape
    hidden_units = gate_weight.shape[1]
    n = lax.axis_size("wide")
    half = width // 2
    rows = n * q_dev
    lists_dev, list_rows, _ = codes.shape
    capacity = (q_dev * PROBES + n - 1) // n
    mib = 1 << 20
    f32, bf16 = jnp.float32, jnp.bfloat16

    def exchange(x):
        return lax.all_to_all(x, "wide", 0, 0, tiled=True)

    def swapped(x, bit):
        return lax.ppermute(x, "wide", [(i, i ^ bit) for i in range(n)])

    gate_near = pltpu.with_memory_space_constraint(gate_weight, VMEM)
    up_near = pltpu.with_memory_space_constraint(up_weight, VMEM)
    down_near = pltpu.with_memory_space_constraint(down_weight, VMEM)
    codes_near = pltpu.with_memory_space_constraint(codes, VMEM)

    hidden_other = swapped(hidden_in, 1)
    probes_other = swapped(probes, 1)
    chip_rows = 2 * q_dev
    normed, rows_here, gain_here = pl.pallas_call(
        norm_kernel,
        out_shape=[
            shaped((q_dev, width + LANES), bf16),
            shaped((q_dev, width), bf16),
            shaped((1, width), f32),
        ],
        in_specs=[pl.BlockSpec(memory_space=pltpu.HBM)] * 3,
        out_specs=[pl.BlockSpec(memory_space=VMEM)] * 3,
        scratch_shapes=[VMEM(probes.shape, jnp.int32), pltpu.SemaphoreType.DMA((3,))],
        compiler_params=pltpu.CompilerParams(vmem_limit_bytes=8 * mib),
        cost_estimate=pl.CostEstimate(flops=1 << 20, bytes_accessed=1 << 20, transcendentals=0),
    )(
        pltpu.with_memory_space_constraint(hidden_in, pltpu.HBM),
        pltpu.with_memory_space_constraint(ffn_gain[None], pltpu.HBM),
        pltpu.with_memory_space_constraint(probes, pltpu.HBM),
    )
    here, residual = call(
        chip_kernel,
        [shaped((chip_rows, half + LANES), bf16), shaped((chip_rows, width), bf16)],
        (normed, rows_here, gain_here, hidden_other, probes_other),
        8 * mib,
        cost=ahead(gate_weight, up_weight, down_weight),
    )
    places = []
    bit = n // 2
    while bit > 2:
        places.append((bit, here.shape[0]))
        here = call(
            join_kernel,
            shaped((2 * here.shape[0], half + LANES), bf16),
            (here, swapped(here, bit)),
            4 * mib,
        )
        bit //= 2
    beyond = swapped(here, 2)
    here_other = swapped(here, 1)
    beyond_other = swapped(beyond, 1)
    gate_part, up_part = call(
        first_kernel,
        [shaped((rows, hidden_units), f32)] * 2,
        (here, beyond, gate_near, up_near, down_near),
        8 * mib,
        cost=products(rows * half * hidden_units * 2),
        scratch=[VMEM((rows, half), bf16)],
    )
    size = half // CHUNKS
    starts = [c * size for c in range(CHUNKS)]
    share = shaped((rows, size), bf16)
    act, sent = call(
        second_kernel,
        [shaped((rows, hidden_units), bf16), share],
        (here_other, beyond_other, gate_part, up_part, gate_near, up_near, down_near),
        8 * mib,
        scratch=[VMEM((rows, half), bf16)],
    )
    came = [swapped(sent, 1)]
    work = products(rows * size * hidden_units)
    for start in starts[1:]:
        sent = call(
            functools.partial(share_kernel, half, start),
            share,
            (act, down_near),
            8 * mib,
            cost=work,
        )
        came.append(swapped(sent, 1))
    side_rows = rows // 2
    kept = [shaped((side_rows, size), f32), shaped((side_rows, size), bf16)]
    keep = []
    for c, start in enumerate(starts):
        own = call(
            functools.partial(own_kernel, half, start),
            shaped((rows, size), f32),
            (act, down_near),
            8 * mib,
            cost=work,
        )
        total, sent = call(
            functools.partial(side_kernel, start), kept, (own, came[c], residual), 8 * mib
        )
        keep.append(total)
        came[c] = swapped(sent, 2)
    move = 0
    for bit, next_move in reversed(places):
        for c in range(CHUNKS):
            keep[c], sent = call(
                functools.partial(sum_kernel, move),
                kept,
                (keep[c], came[c]),
                8 * mib,
                cost=ahead(codes) if move == 0 and c == 0 else None,
            )
            came[c] = swapped(sent, bit)
        move = next_move
    route = call(
        functools.partial(route_kernel, lists_dev, capacity),
        shaped((n * capacity, LANES), jnp.int32),
        (probes, list_slot[None], counts[None], keep[-1]),
        4 * mib,
    )
    wanted = call(
        functools.partial(wanted_kernel, capacity, q_dev, PROBES, n, tuple(places)),
        shaped((n * capacity, LANES), jnp.int32),
        (here, beyond, list_slot[None], route),
        4 * mib,
    )
    near = [
        call(
            functools.partial(scale_kernel, start, move),
            shaped((side_rows, size + LANES), bf16),
            (keep[c], came[c], final_gain[None], wanted),
            8 * mib,
        )
        for c, start in enumerate(starts)
    ]
    far = []
    for x in near:
        far.append(swapped(x, 2))
    near_other = [swapped(x, 1) for x in near]
    far_other = [swapped(x, 1) for x in far]
    scales_near = jnp.swapaxes(scales, 1, 2)
    pairs = n * capacity
    sofar = []
    for c, start in enumerate(starts):
        sofar = call(
            functools.partial(some_scores_kernel, True, start),
            [shaped((pairs, list_rows), f32), shaped((pairs, LANES), f32)],
            (near[c], far[c], wanted, codes_near, scales_near, *sofar),
            8 * mib,
            cost=products(pairs * lists_dev * list_rows * size),
            scratch=[VMEM((pairs, size), bf16), VMEM((2 * pairs, size), bf16)],
        )
    others = [x for pair in zip(near_other, far_other) for x in pair]
    scores = call(
        functools.partial(last_scores_kernel, False, starts),
        shaped((n, capacity, list_rows), f32),
        (*others, wanted, codes_near, scales_near, *sofar),
        8 * mib,
        scratch=[VMEM((CHUNKS, pairs, size), bf16), VMEM((CHUNKS, 2 * pairs, size), bf16)],
    )
    back = exchange(scores)
    return call(best_kernel, shaped((q_dev, K_TOP), f32), (back, route), 8 * mib)


def solution(mesh):
    in_specs = (
        P(("grp", "wide"), None),
        P(),
        P(None, "wide"),
        P(None, "wide"),
        P("wide", None),
        P(),
        P(("grp", "wide"), None, None),
        P(("grp", "wide"), None, None),
        P("grp"),
        P("grp"),
        P(("grp", "wide"), None),
    )
    out_specs = P(("grp", "wide"), None)
    return jax.shard_map(body, mesh=mesh, in_specs=in_specs, out_specs=out_specs, check_vma=False)
```

```python
import functools

import jax
import jax.numpy as jnp
from jax import lax
from jax.experimental import pallas as pl
from jax.experimental.pallas import tpu as pltpu
from jax.sharding import PartitionSpec as P


PROBES = 8
K_TOP = 8
BLOCK = 128
LANES = 128
SUBLANES = 8
DIGIT = 256
CHUNKS = 2


floor_score = -1e30

VMEM = pltpu.VMEM


def call(kernel, out_shape, args, vmem, cost=None, scratch=()):
    many = isinstance(out_shape, (list, tuple))
    return pl.pallas_call(
        kernel,
        out_shape=out_shape,
        in_specs=[pl.BlockSpec(memory_space=VMEM)] * len(args),
        out_specs=[pl.BlockSpec(memory_space=VMEM)] * len(out_shape)
        if many
        else pl.BlockSpec(memory_space=VMEM),
        scratch_shapes=list(scratch),
        compiler_params=pltpu.CompilerParams(vmem_limit_bytes=vmem),
        cost_estimate=cost,
    )(*args)


def ahead(*arrays):
    total = sum(a.size * a.dtype.itemsize for a in arrays)
    return pl.CostEstimate(flops=1000 * total, bytes_accessed=1 << 20, transcendentals=0)


def products(count):
    return pl.CostEstimate(flops=2 * count, bytes_accessed=1 << 20, transcendentals=0)


def shaped(shape, dtype):
    return jax.ShapeDtypeStruct(shape, dtype)


def norm_kernel(hidden_ref, gain_ref, probes_ref, out_ref, rows_ref, scale_ref, ids_ref, sems):
    copies = [
        pltpu.make_async_copy(source, target, sems.at[index])
        for index, (source, target) in enumerate(
            [(hidden_ref, rows_ref), (gain_ref, scale_ref), (probes_ref, ids_ref)]
        )
    ]
    for copy in copies:
        copy.start()
    for copy in copies:
        copy.wait()
    rows = rows_ref[...].astype(jnp.float32)
    width = rows.shape[1]
    scale = lax.rsqrt(jnp.mean(rows * rows, axis=-1, keepdims=True) + 1e-05)
    out_ref[:, :width] = (rows * scale * scale_ref[...]).astype(jnp.bfloat16)

    q_dev, probes = ids_ref.shape
    pairs = q_dev * probes
    lane = lax.broadcasted_iota(jnp.int32, (q_dev, LANES), 1)
    query = lax.broadcasted_iota(jnp.int32, (q_dev, LANES), 0)
    ids = jnp.zeros((q_dev, LANES), jnp.int32)
    for j in range(probes):
        ids = jnp.where(lane % probes == j, ids_ref[:, j : j + 1], ids)
    ids = jnp.where((lane % pairs) // probes == query, ids, 0)
    ids = jnp.sum(ids, axis=0, keepdims=True)
    digits = jnp.where(lane < pairs, ids // DIGIT, ids % DIGIT)
    digits = jnp.where(lane < 2 * pairs, digits, 0)
    out_ref[:, width:] = digits.astype(jnp.float32).astype(jnp.bfloat16)


def spread_kernel(normed_ref, out_ref):
    half = out_ref.shape[2] - LANES
    for k in range(out_ref.shape[0]):
        core = k % 2
        out_ref[k, :, :half] = normed_ref[:, core * half : (core + 1) * half]
        out_ref[k, :, half:] = normed_ref[:, 2 * half :]


def wanted_kernel(capacity, q_dev, probes, here_ref, slot_ref, after_ref, out_ref):
    devices, _, wide = here_ref.shape
    half = wide - LANES
    lists = slot_ref.shape[1]
    pairs = q_dev * probes
    lists_dev = lists // devices
    me = lax.axis_index("wide")
    tails = here_ref[:, :, half:].astype(jnp.float32)
    tails = jnp.max(tails, axis=1).astype(jnp.int32)
    ids = tails[:, :pairs] * DIGIT + tails[:, pairs : 2 * pairs]
    number = lax.broadcasted_iota(jnp.int32, (1, lists), 1)
    local = jnp.full((devices, pairs), -1, jnp.int32)
    for index in range(lists_dev):
        held = slot_ref[...] == me * lists_dev + index
        mine = jnp.sum(jnp.where(held, number, 0), axis=1, keepdims=True)
        local = jnp.where(ids == mine, index, local)
    pair = lax.broadcasted_iota(jnp.int32, (devices, pairs), 1)
    home = lax.broadcasted_iota(jnp.int32, (devices, 1), 0)
    place = lax.broadcasted_iota(jnp.int32, (devices, LANES), 1)
    side = lax.rem(me, 4) // 2
    before = jnp.full((devices, 1), -1, jnp.int32)
    for rank in range(capacity):
        open_pair = (local >= 0) & (pair > before)
        chosen = jnp.min(jnp.where(open_pair, pair, pairs), axis=1, keepdims=True)
        there = jnp.sum(jnp.where(pair == chosen, local, 0), axis=1, keepdims=True)
        row = jnp.where(
            lax.rem(home, 4) // 2 == side, 0, devices * q_dev // 2
        ) + home // 4 * (2 * q_dev) + lax.rem(home, 2) * q_dev + chosen // probes
        row = jnp.where(chosen < pairs, row, -1)
        out_ref[rank * devices : (rank + 1) * devices, :] = jnp.where(
            place == 0, row, jnp.where(place == 1, there, 0)
        )
        before = chosen


def route_kernel(lists_dev, capacity, probes_ref, slot_ref, count_ref, after_ref, out_ref):
    q_dev, probes = probes_ref.shape
    lists = slot_ref.shape[1]
    pairs = q_dev * probes
    slots = out_ref.shape[0]
    ids = jnp.concatenate(
        [jnp.broadcast_to(probes_ref[q : q + 1, :], (probes, probes)) for q in range(q_dev)], axis=0
    )
    sub = lax.broadcasted_iota(jnp.int32, (pairs, probes), 0)
    lane = lax.broadcasted_iota(jnp.int32, (pairs, probes), 1)
    ids = jnp.sum(jnp.where(sub % probes == lane, ids, 0), axis=1, keepdims=True)
    hit = lax.broadcasted_iota(jnp.int32, (pairs, lists), 1) == ids
    slot = jnp.sum(jnp.where(hit, slot_ref[...], 0), axis=1, keepdims=True)
    valid = jnp.sum(jnp.where(hit, count_ref[...], 0), axis=1, keepdims=True)
    owner = slot // lists_dev
    local = slot % lists_dev
    p_sub = lax.broadcasted_iota(jnp.int32, (pairs, pairs), 0)
    p_lane = lax.broadcasted_iota(jnp.int32, (pairs, pairs), 1)
    diagonal = p_sub == p_lane

    def as_row(column):
        return jnp.sum(jnp.where(diagonal, column, 0), axis=0, keepdims=True)

    owner_row = as_row(owner)
    rank_row = jnp.sum(
        jnp.where((owner == owner_row) & (p_sub < p_lane), 1, 0), axis=0, keepdims=True
    )
    target_row = owner_row * capacity + rank_row
    here = lax.broadcasted_iota(jnp.int32, (slots, pairs), 0) == target_row
    pair_row = lax.broadcasted_iota(jnp.int32, (slots, pairs), 1)

    def of_slot(row):
        return jnp.sum(jnp.where(here, row, 0), axis=1, keepdims=True)

    query = of_slot(pair_row // probes + 1) - 1
    place = lax.broadcasted_iota(jnp.int32, (slots, LANES), 1)
    out = jnp.where(place == 0, query, 0)
    out = jnp.where(place == 1, of_slot(as_row(local)), out)
    out_ref[...] = jnp.where(place == 2, of_slot(as_row(valid)), out)


def my_span(mine, half, start, size):
    core = lax.rem(lax.axis_index("wide"), 2)
    which = core if mine else 1 - core
    return pl.ds(pl.multiple_of(which * half + start, size), size)


def first_kernel(here_ref, gate_ref, up_ref, after_ref, gate_out, up_out, rows_ref):
    rows_ref[...] = here_ref[:, :, : rows_ref.shape[1]].reshape(rows_ref.shape)
    half = rows_ref.shape[1]
    span = my_span(True, half, 0, half)
    gate_out[...] = jnp.dot(rows_ref[...], gate_ref[span, :], preferred_element_type=jnp.float32)
    up_out[...] = jnp.dot(rows_ref[...], up_ref[span, :], preferred_element_type=jnp.float32)


def put_share(act_ref, down_ref, hidden_ref, send_ref, half, start):
    rows, size = act_ref.shape[0], send_ref.shape[1]
    span = my_span(False, half, start, size)
    send_ref[:rows, :] = jnp.dot(
        act_ref[...], down_ref[:, span], preferred_element_type=jnp.float32
    ).astype(jnp.bfloat16)
    residual = hidden_ref[:, span]
    send_ref[rows:, :] = jnp.concatenate([residual, residual], axis=0)


def second_kernel(
    there_ref, gate_part, up_part, gate_ref, up_ref, down_ref, hidden_ref, act_ref, send_ref, rows_ref
):
    half = rows_ref.shape[1]
    rows_ref[...] = there_ref[:, :, :half].reshape(rows_ref.shape)
    span = my_span(False, half, 0, half)
    gate = gate_part[...] + jnp.dot(
        rows_ref[...], gate_ref[span, :], preferred_element_type=jnp.float32
    )
    up = up_part[...] + jnp.dot(
        rows_ref[...], up_ref[span, :], preferred_element_type=jnp.float32
    )
    act_ref[...] = (gate / (1.0 + jnp.exp(-gate)) * up).astype(jnp.bfloat16)
    put_share(act_ref, down_ref, hidden_ref, send_ref, half, 0)


def share_kernel(half, start, act_ref, down_ref, hidden_ref, send_ref):
    put_share(act_ref, down_ref, hidden_ref, send_ref, half, start)


def own_kernel(half, start, act_ref, down_ref, own_ref):
    span = my_span(True, half, start, own_ref.shape[1])
    own_ref[...] = jnp.dot(act_ref[...], down_ref[:, span], preferred_element_type=jnp.float32)


def side_kernel(start, own_ref, came_ref, hidden_ref, keep_ref, send_ref):
    rows, size = own_ref.shape
    q_dev, width = hidden_ref.shape
    half = width // 2
    me = lax.axis_index("wide")
    core, side, plane = lax.rem(me, 2), lax.rem(me, 4) // 2, me // 4
    group = 2 * q_dev
    mine = jnp.where(
        core == 0,
        hidden_ref[:, start : start + size],
        hidden_ref[:, half + start : half + start + size],
    ).astype(jnp.float32)
    other = came_ref[rows : rows + q_dev, :].astype(jnp.float32)
    residual = jnp.where(
        core == 0,
        jnp.concatenate([mine, other], axis=0),
        jnp.concatenate([other, mine], axis=0),
    )
    for z in range(rows // (2 * group)):
        total = []
        for y in range(2):
            span = slice((2 * z + y) * group, (2 * z + y + 1) * group)
            total.append(own_ref[span, :] + came_ref[span, :].astype(jnp.float32))
        kept = jnp.where(side == 0, total[0], total[1])
        sent = jnp.where(side == 0, total[1], total[0])
        span = slice(z * group, (z + 1) * group)
        keep_ref[span, :] = kept + jnp.where(plane == z, residual, jnp.zeros_like(residual))
        send_ref[span, :] = sent.astype(jnp.bfloat16)


def sum_kernel(keep_ref, came_ref, total_ref, send_ref):
    total = keep_ref[...] + came_ref[...].astype(jnp.float32)
    total_ref[...] = total
    send_ref[...] = total.astype(jnp.bfloat16)


def scale_kernel(start, keep_ref, came_ref, gain_ref, after_ref, out_ref):
    rows, size = keep_ref.shape
    half = gain_ref.shape[1] // 2
    core = lax.rem(lax.axis_index("wide"), 2)
    gain = jnp.where(
        core == 0,
        gain_ref[:, start : start + size],
        gain_ref[:, half + start : half + start + size],
    )
    scaled = gain * (keep_ref[...] + came_ref[...].astype(jnp.float32))
    out_ref[:, :size] = scaled.astype(jnp.bfloat16)
    left = jnp.sum(scaled * scaled, axis=-1, keepdims=True)
    lane = lax.broadcasted_iota(jnp.int32, (rows, LANES), 1)
    tail = jnp.zeros((rows, LANES), jnp.float32)
    for piece in range(3):
        part = left.astype(jnp.bfloat16).astype(jnp.float32)
        tail = jnp.where(lane == piece, part, tail)
        left = left - part
    out_ref[:, size:] = tail.astype(jnp.bfloat16)


def chunk_scores(
    mine, start, near_ref, far_ref, wanted_ref, codes_ref, scales_ref, picks_ref, rows_ref
):
    side_rows, wide = near_ref.shape
    size = wide - LANES
    lists, list_rows, width = codes_ref.shape
    half = width // 2
    pairs = wanted_ref.shape[0]
    row = wanted_ref[:, 0:1]
    local = wanted_ref[:, 1:2]
    column = lax.broadcasted_iota(jnp.int32, (pairs, side_rows), 1)

    def pick(ref, first):
        hot = jnp.where(column + first == row, 1.0, 0.0).astype(jnp.bfloat16)
        return jnp.dot(hot, ref[...], preferred_element_type=jnp.float32)

    chosen = pick(near_ref, 0) + pick(far_ref, side_rows)
    picks_ref[...] = chosen[:, :size].astype(jnp.bfloat16)
    nothing = jnp.zeros((pairs, BLOCK), jnp.bfloat16)
    for block in range(size // BLOCK):
        span = slice(block * BLOCK, (block + 1) * BLOCK)
        kept = block % 2
        rows_ref[kept * pairs : (kept + 1) * pairs, span] = picks_ref[:, span]
        rows_ref[(1 - kept) * pairs : (2 - kept) * pairs, span] = nothing
    squares = jnp.sum(chosen[:, size:], axis=1, keepdims=True)

    core = lax.rem(lax.axis_index("wide"), 2)
    which = core if mine else 1 - core
    blocks = size // BLOCK
    here = pl.ds(
        pl.multiple_of(which * (half // BLOCK) + start // BLOCK, blocks), blocks
    )
    picked = jnp.zeros((pairs, list_rows), jnp.float32)
    for first in range(0, lists, 2):
        scale = jnp.concatenate([scales_ref[first, here, :], scales_ref[first + 1, here, :]], axis=1)
        total = jnp.zeros((pairs, 2 * list_rows), jnp.float32)
        for step in range(blocks // 2):
            span = slice(step * 2 * BLOCK, (step + 1) * 2 * BLOCK)
            away = my_span(mine, half, start + step * 2 * BLOCK, 2 * BLOCK)
            part = lax.dot_general(
                rows_ref[:, span],
                codes_ref[first : first + 2, :, away].reshape(2 * list_rows, 2 * BLOCK),
                (((1,), (1,)), ((), ())),
                preferred_element_type=jnp.float32,
            )
            total += part[:pairs] * scale[2 * step : 2 * step + 1, :]
            total += part[pairs:] * scale[2 * step + 1 : 2 * step + 2, :]
        picked = jnp.where(local == first, total[:, :list_rows], picked)
        picked = jnp.where(local == first + 1, total[:, list_rows:], picked)
    return picked, squares


def some_scores_kernel(
    mine, start, near_ref, far_ref, wanted_ref, codes_ref, scales_ref, *rest
):
    *sofar, picked_ref, squares_ref, picks_ref, rows_ref = rest
    picked, squares = chunk_scores(
        mine, start, near_ref, far_ref, wanted_ref, codes_ref, scales_ref, picks_ref, rows_ref
    )
    if sofar:
        picked += sofar[0][...]
        squares = squares + sofar[1][...]
    picked_ref[...] = picked
    squares_ref[...] = jnp.broadcast_to(squares, squares_ref.shape)


def last_scores_kernel(mine, starts, *refs):
    chunks = len(starts)
    tables = refs[2 * chunks : 2 * chunks + 3]
    sofar_ref, squares_ref, out_ref, picks_ref, rows_ref = refs[2 * chunks + 3 :]
    scores, squares = sofar_ref[...], squares_ref[:, 0:1]
    for c, start in enumerate(starts):
        picked, more = chunk_scores(
            mine, start, refs[2 * c], refs[2 * c + 1], *tables, picks_ref.at[c], rows_ref.at[c]
        )
        scores += picked
        squares = squares + more
    scores = scores * lax.rsqrt(squares + 1e-06)
    devices, capacity, _ = out_ref.shape
    for rank in range(capacity):
        out_ref[:, rank, :] = scores[rank * devices : (rank + 1) * devices]


def sort_merged(a):
    step = len(a) // 2
    while step:
        for i in range(len(a)):
            if i % (2 * step) < step:
                a[i], a[i + step] = jnp.maximum(a[i], a[i + step]), jnp.minimum(a[i], a[i + step])
        step //= 2
    return a


def best_kernel(back_ref, route_ref, out_ref):
    q_dev, count = out_ref.shape
    sources, slots, list_rows = back_ref.shape
    pairs = sources * slots
    scores = back_ref[...].reshape(pairs, list_rows)
    query = route_ref[:, 0:1]
    alive = lax.broadcasted_iota(jnp.int32, (pairs, list_rows), 1) < route_ref[:, 2:3]
    lists = []
    for q in range(q_dev):
        left = jnp.where(alive & (query == q), scores, floor_score)
        tiles = [[left[start : start + SUBLANES]] for start in range(0, pairs, SUBLANES)]
        while len(tiles) > 1:
            merged = [
                sort_merged(one + two[::-1]) for one, two in zip(tiles[::2], tiles[1::2])
            ]
            tiles = [a[:count] for a in merged]
        a = tiles[0]
        shift = SUBLANES // 2
        while shift:
            b = [pltpu.roll(v, shift, 0) for v in a][::-1]
            if 2 * len(a) <= count:
                a = sort_merged(a + b)
            else:
                a = sort_merged([jnp.maximum(one, two) for one, two in zip(a, b)])
            shift //= 2
        lists.append(a)
    place = lax.broadcasted_iota(jnp.int32, (SUBLANES, list_rows), 0)
    a = []
    for rank in range(count):
        v = lists[0][rank]
        for q in range(1, q_dev):
            v = jnp.where(place == q, lists[q][rank], v)
        a.append(v)
    shift = list_rows // 2
    while shift:
        b = [pltpu.roll(v, shift, 1) for v in a][::-1]
        a = sort_merged([jnp.maximum(one, two) for one, two in zip(a, b)])
        shift //= 2
    lane = lax.broadcasted_iota(jnp.int32, (SUBLANES, list_rows), 1)
    out = a[0]
    for rank in range(1, count):
        out = jnp.where(lane == rank, a[rank], out)
    out_ref[...] = out[:q_dev, :count]


def body(
    hidden_in,
    ffn_gain,
    gate_weight,
    up_weight,
    down_weight,
    final_gain,
    codes,
    scales,
    counts,
    list_slot,
    probes,
):
    q_dev, width = hidden_in.shape
    hidden_units = gate_weight.shape[1]
    n = lax.axis_size("wide")
    half = width // 2
    rows = n * q_dev
    lists_dev, list_rows, _ = codes.shape
    capacity = (q_dev * PROBES + n - 1) // n
    mib = 1 << 20
    f32, bf16 = jnp.float32, jnp.bfloat16

    def exchange(x):
        return lax.all_to_all(x, "wide", 0, 0, tiled=True)

    def swapped(x, bit):
        return lax.ppermute(x, "wide", [(i, i ^ bit) for i in range(n)])

    gate_near = pltpu.with_memory_space_constraint(gate_weight, VMEM)
    up_near = pltpu.with_memory_space_constraint(up_weight, VMEM)
    down_near = pltpu.with_memory_space_constraint(down_weight, VMEM)
    codes_near = pltpu.with_memory_space_constraint(codes, VMEM)

    normed = pl.pallas_call(
        norm_kernel,
        out_shape=shaped((q_dev, width + LANES), bf16),
        in_specs=[pl.BlockSpec(memory_space=pltpu.HBM)] * 3,
        out_specs=pl.BlockSpec(memory_space=VMEM),
        scratch_shapes=[
            VMEM((q_dev, width), bf16),
            VMEM((1, width), f32),
            VMEM(probes.shape, jnp.int32),
            pltpu.SemaphoreType.DMA((3,)),
        ],
        compiler_params=pltpu.CompilerParams(vmem_limit_bytes=8 * mib),
    )(
        pltpu.with_memory_space_constraint(hidden_in, pltpu.HBM),
        pltpu.with_memory_space_constraint(ffn_gain[None], pltpu.HBM),
        pltpu.with_memory_space_constraint(probes, pltpu.HBM),
    )
    spread = call(
        spread_kernel,
        shaped((n, q_dev, half + LANES), bf16),
        (normed,),
        8 * mib,
        cost=ahead(gate_weight, up_weight, down_weight),
    )
    here = exchange(spread)
    there = swapped(here, 1)
    gate_part, up_part = call(
        first_kernel,
        [shaped((rows, hidden_units), f32)] * 2,
        (here, gate_near, up_near, down_near),
        8 * mib,
        cost=products(rows * half * hidden_units * 2),
        scratch=[VMEM((rows, half), bf16)],
    )
    size = half // CHUNKS
    starts = [c * size for c in range(CHUNKS)]
    share = shaped((rows + 2 * q_dev, size), bf16)
    act, sent = call(
        second_kernel,
        [shaped((rows, hidden_units), bf16), share],
        (there, gate_part, up_part, gate_near, up_near, down_near, hidden_in),
        8 * mib,
        scratch=[VMEM((rows, half), bf16)],
    )
    came = [swapped(sent, 1)]
    work = products(rows * size * hidden_units)
    for start in starts[1:]:
        sent = call(
            functools.partial(share_kernel, half, start),
            share,
            (act, down_near, hidden_in),
            8 * mib,
            cost=work,
        )
        came.append(swapped(sent, 1))
    side_rows = rows // 2
    kept = [shaped((side_rows, size), f32), shaped((side_rows, size), bf16)]
    keep = []
    for c, start in enumerate(starts):
        own = call(
            functools.partial(own_kernel, half, start),
            shaped((rows, size), f32),
            (act, down_near),
            8 * mib,
            cost=work,
        )
        total, sent = call(
            functools.partial(side_kernel, start), kept, (own, came[c], hidden_in), 8 * mib
        )
        keep.append(total)
        came[c] = swapped(sent, 2)
    bit = 4
    while bit < n:
        for c in range(CHUNKS):
            keep[c], sent = call(
                sum_kernel,
                kept,
                (keep[c], came[c]),
                8 * mib,
                cost=ahead(codes) if bit == 4 and c == 0 else None,
            )
            came[c] = swapped(sent, bit)
        bit *= 2
    route = call(
        functools.partial(route_kernel, lists_dev, capacity),
        shaped((n * capacity, LANES), jnp.int32),
        (probes, list_slot[None], counts[None], keep[-1]),
        4 * mib,
    )
    wanted = call(
        functools.partial(wanted_kernel, capacity, q_dev, PROBES),
        shaped((n * capacity, LANES), jnp.int32),
        (here, list_slot[None], route),
        4 * mib,
    )
    near = [
        call(
            functools.partial(scale_kernel, start),
            shaped((side_rows, size + LANES), bf16),
            (keep[c], came[c], final_gain[None], wanted),
            8 * mib,
        )
        for c, start in enumerate(starts)
    ]
    far = []
    for x in near:
        far.append(swapped(x, 2))
    near_other = [swapped(x, 1) for x in near]
    far_other = []
    for x in far:
        far_other.append(swapped(x, 1))
    scales_near = jnp.swapaxes(scales, 1, 2)
    pairs = n * capacity
    sofar = []
    for c, start in enumerate(starts):
        sofar = call(
            functools.partial(some_scores_kernel, True, start),
            [shaped((pairs, list_rows), f32), shaped((pairs, LANES), f32)],
            (near[c], far[c], wanted, codes_near, scales_near, *sofar),
            8 * mib,
            cost=products(pairs * lists_dev * list_rows * size),
            scratch=[VMEM((pairs, size), bf16), VMEM((2 * pairs, size), bf16)],
        )
    others = [x for pair in zip(near_other, far_other) for x in pair]
    scores = call(
        functools.partial(last_scores_kernel, False, starts),
        shaped((n, capacity, list_rows), f32),
        (*others, wanted, codes_near, scales_near, *sofar),
        8 * mib,
        scratch=[VMEM((CHUNKS, pairs, size), bf16), VMEM((CHUNKS, 2 * pairs, size), bf16)],
    )
    back = exchange(scores)
    return call(best_kernel, shaped((q_dev, K_TOP), f32), (back, route), 8 * mib)


def solution(mesh):
    in_specs = (
        P(("grp", "wide"), None),
        P(),
        P(None, "wide"),
        P(None, "wide"),
        P("wide", None),
        P(),
        P(("grp", "wide"), None, None),
        P(("grp", "wide"), None, None),
        P("grp"),
        P("grp"),
        P(("grp", "wide"), None),
    )
    out_specs = P(("grp", "wide"), None)
    return jax.shard_map(body, mesh=mesh, in_specs=in_specs, out_specs=out_specs, check_vma=False)
```

```python
import functools

import jax
import jax.numpy as jnp
from jax import lax
from jax.experimental import pallas as pl
from jax.experimental.pallas import tpu as pltpu
from jax.sharding import PartitionSpec as P


PROBES = 8
K_TOP = 8
BLOCK = 128
LANES = 128
SUBLANES = 8
DIGIT = 256
CHUNKS = 2


floor_score = -1e30

VMEM = pltpu.VMEM


def call(kernel, out_shape, args, vmem, cost=None, scratch=()):
    many = isinstance(out_shape, (list, tuple))
    return pl.pallas_call(
        kernel,
        out_shape=out_shape,
        in_specs=[pl.BlockSpec(memory_space=VMEM)] * len(args),
        out_specs=[pl.BlockSpec(memory_space=VMEM)] * len(out_shape)
        if many
        else pl.BlockSpec(memory_space=VMEM),
        scratch_shapes=list(scratch),
        compiler_params=pltpu.CompilerParams(vmem_limit_bytes=vmem),
        cost_estimate=cost,
    )(*args)


def ahead(*arrays):
    total = sum(a.size * a.dtype.itemsize for a in arrays)
    return pl.CostEstimate(flops=1000 * total, bytes_accessed=1 << 20, transcendentals=0)


def products(count):
    return pl.CostEstimate(flops=2 * count, bytes_accessed=1 << 20, transcendentals=0)


def shaped(shape, dtype):
    return jax.ShapeDtypeStruct(shape, dtype)


def norm_kernel(hidden_ref, gain_ref, probes_ref, out_ref, rows_ref, scale_ref, ids_ref, sems):
    copies = [
        pltpu.make_async_copy(source, target, sems.at[index])
        for index, (source, target) in enumerate(
            [(hidden_ref, rows_ref), (gain_ref, scale_ref), (probes_ref, ids_ref)]
        )
    ]
    for copy in copies:
        copy.start()
    for copy in copies:
        copy.wait()
    rows = rows_ref[...].astype(jnp.float32)
    width = rows.shape[1]
    scale = lax.rsqrt(jnp.mean(rows * rows, axis=-1, keepdims=True) + 1e-05)
    out_ref[:, :width] = (rows * scale * scale_ref[...]).astype(jnp.bfloat16)

    q_dev, probes = ids_ref.shape
    pairs = q_dev * probes
    lane = lax.broadcasted_iota(jnp.int32, (q_dev, LANES), 1)
    query = lax.broadcasted_iota(jnp.int32, (q_dev, LANES), 0)
    ids = jnp.zeros((q_dev, LANES), jnp.int32)
    for j in range(probes):
        ids = jnp.where(lane % probes == j, ids_ref[:, j : j + 1], ids)
    ids = jnp.where((lane % pairs) // probes == query, ids, 0)
    ids = jnp.sum(ids, axis=0, keepdims=True)
    digits = jnp.where(lane < pairs, ids // DIGIT, ids % DIGIT)
    digits = jnp.where(lane < 2 * pairs, digits, 0)
    out_ref[:, width:] = digits.astype(jnp.float32).astype(jnp.bfloat16)


def spread_kernel(normed_ref, out_ref):
    half = out_ref.shape[2] - LANES
    for k in range(out_ref.shape[0]):
        core = k % 2
        out_ref[k, :, :half] = normed_ref[:, core * half : (core + 1) * half]
        out_ref[k, :, half:] = normed_ref[:, 2 * half :]


def wanted_kernel(capacity, q_dev, probes, here_ref, slot_ref, after_ref, out_ref):
    devices, _, wide = here_ref.shape
    half = wide - LANES
    lists = slot_ref.shape[1]
    pairs = q_dev * probes
    lists_dev = lists // devices
    me = lax.axis_index("wide")
    tails = here_ref[:, :, half:].astype(jnp.float32)
    tails = jnp.max(tails, axis=1).astype(jnp.int32)
    ids = tails[:, :pairs] * DIGIT + tails[:, pairs : 2 * pairs]
    number = lax.broadcasted_iota(jnp.int32, (1, lists), 1)
    local = jnp.full((devices, pairs), -1, jnp.int32)
    for index in range(lists_dev):
        held = slot_ref[...] == me * lists_dev + index
        mine = jnp.sum(jnp.where(held, number, 0), axis=1, keepdims=True)
        local = jnp.where(ids == mine, index, local)
    pair = lax.broadcasted_iota(jnp.int32, (devices, pairs), 1)
    home = lax.broadcasted_iota(jnp.int32, (devices, 1), 0)
    place = lax.broadcasted_iota(jnp.int32, (devices, LANES), 1)
    side = lax.rem(me, 4) // 2
    before = jnp.full((devices, 1), -1, jnp.int32)
    for rank in range(capacity):
        open_pair = (local >= 0) & (pair > before)
        chosen = jnp.min(jnp.where(open_pair, pair, pairs), axis=1, keepdims=True)
        there = jnp.sum(jnp.where(pair == chosen, local, 0), axis=1, keepdims=True)
        row = jnp.where(
            lax.rem(home, 4) // 2 == side, 0, devices * q_dev // 2
        ) + home // 4 * (2 * q_dev) + lax.rem(home, 2) * q_dev + chosen // probes
        row = jnp.where(chosen < pairs, row, -1)
        out_ref[rank * devices : (rank + 1) * devices, :] = jnp.where(
            place == 0, row, jnp.where(place == 1, there, 0)
        )
        before = chosen


def route_kernel(lists_dev, capacity, probes_ref, slot_ref, count_ref, after_ref, out_ref):
    q_dev, probes = probes_ref.shape
    lists = slot_ref.shape[1]
    pairs = q_dev * probes
    slots = out_ref.shape[0]
    ids = jnp.concatenate(
        [jnp.broadcast_to(probes_ref[q : q + 1, :], (probes, probes)) for q in range(q_dev)], axis=0
    )
    sub = lax.broadcasted_iota(jnp.int32, (pairs, probes), 0)
    lane = lax.broadcasted_iota(jnp.int32, (pairs, probes), 1)
    ids = jnp.sum(jnp.where(sub % probes == lane, ids, 0), axis=1, keepdims=True)
    hit = lax.broadcasted_iota(jnp.int32, (pairs, lists), 1) == ids
    slot = jnp.sum(jnp.where(hit, slot_ref[...], 0), axis=1, keepdims=True)
    valid = jnp.sum(jnp.where(hit, count_ref[...], 0), axis=1, keepdims=True)
    owner = slot // lists_dev
    local = slot % lists_dev
    p_sub = lax.broadcasted_iota(jnp.int32, (pairs, pairs), 0)
    p_lane = lax.broadcasted_iota(jnp.int32, (pairs, pairs), 1)
    diagonal = p_sub == p_lane

    def as_row(column):
        return jnp.sum(jnp.where(diagonal, column, 0), axis=0, keepdims=True)

    owner_row = as_row(owner)
    rank_row = jnp.sum(
        jnp.where((owner == owner_row) & (p_sub < p_lane), 1, 0), axis=0, keepdims=True
    )
    target_row = owner_row * capacity + rank_row
    here = lax.broadcasted_iota(jnp.int32, (slots, pairs), 0) == target_row
    pair_row = lax.broadcasted_iota(jnp.int32, (slots, pairs), 1)

    def of_slot(row):
        return jnp.sum(jnp.where(here, row, 0), axis=1, keepdims=True)

    query = of_slot(pair_row // probes + 1) - 1
    place = lax.broadcasted_iota(jnp.int32, (slots, LANES), 1)
    out = jnp.where(place == 0, query, 0)
    out = jnp.where(place == 1, of_slot(as_row(local)), out)
    out_ref[...] = jnp.where(place == 2, of_slot(as_row(valid)), out)


def my_span(mine, half, start, size):
    core = lax.rem(lax.axis_index("wide"), 2)
    which = core if mine else 1 - core
    return pl.ds(pl.multiple_of(which * half + start, size), size)


def first_kernel(here_ref, gate_ref, up_ref, after_ref, gate_out, up_out, rows_ref):
    rows_ref[...] = here_ref[:, :, : rows_ref.shape[1]].reshape(rows_ref.shape)
    half = rows_ref.shape[1]
    span = my_span(True, half, 0, half)
    gate_out[...] = jnp.dot(rows_ref[...], gate_ref[span, :], preferred_element_type=jnp.float32)
    up_out[...] = jnp.dot(rows_ref[...], up_ref[span, :], preferred_element_type=jnp.float32)


def put_share(act_ref, down_ref, hidden_ref, send_ref, half, start):
    rows, size = act_ref.shape[0], send_ref.shape[1]
    span = my_span(False, half, start, size)
    send_ref[:rows, :] = jnp.dot(
        act_ref[...], down_ref[:, span], preferred_element_type=jnp.float32
    ).astype(jnp.bfloat16)
    residual = hidden_ref[:, span]
    send_ref[rows:, :] = jnp.concatenate([residual, residual], axis=0)


def second_kernel(
    there_ref, gate_part, up_part, gate_ref, up_ref, down_ref, hidden_ref, act_ref, send_ref, rows_ref
):
    half = rows_ref.shape[1]
    rows_ref[...] = there_ref[:, :, :half].reshape(rows_ref.shape)
    span = my_span(False, half, 0, half)
    gate = gate_part[...] + jnp.dot(
        rows_ref[...], gate_ref[span, :], preferred_element_type=jnp.float32
    )
    up = up_part[...] + jnp.dot(
        rows_ref[...], up_ref[span, :], preferred_element_type=jnp.float32
    )
    act_ref[...] = (gate / (1.0 + jnp.exp(-gate)) * up).astype(jnp.bfloat16)
    put_share(act_ref, down_ref, hidden_ref, send_ref, half, 0)


def share_kernel(half, start, act_ref, down_ref, hidden_ref, after_ref, send_ref):
    put_share(act_ref, down_ref, hidden_ref, send_ref, half, start)


def own_kernel(half, start, act_ref, down_ref, own_ref):
    span = my_span(True, half, start, own_ref.shape[1])
    own_ref[...] = jnp.dot(act_ref[...], down_ref[:, span], preferred_element_type=jnp.float32)


def side_kernel(start, own_ref, came_ref, hidden_ref, keep_ref, send_ref):
    rows, size = own_ref.shape
    q_dev, width = hidden_ref.shape
    half = width // 2
    me = lax.axis_index("wide")
    core, side, plane = lax.rem(me, 2), lax.rem(me, 4) // 2, me // 4
    group = 2 * q_dev
    mine = jnp.where(
        core == 0,
        hidden_ref[:, start : start + size],
        hidden_ref[:, half + start : half + start + size],
    ).astype(jnp.float32)
    other = came_ref[rows : rows + q_dev, :].astype(jnp.float32)
    residual = jnp.where(
        core == 0,
        jnp.concatenate([mine, other], axis=0),
        jnp.concatenate([other, mine], axis=0),
    )
    for z in range(rows // (2 * group)):
        total = []
        for y in range(2):
            span = slice((2 * z + y) * group, (2 * z + y + 1) * group)
            total.append(own_ref[span, :] + came_ref[span, :].astype(jnp.float32))
        kept = jnp.where(side == 0, total[0], total[1])
        sent = jnp.where(side == 0, total[1], total[0])
        span = slice(z * group, (z + 1) * group)
        keep_ref[span, :] = kept + jnp.where(plane == z, residual, jnp.zeros_like(residual))
        send_ref[span, :] = sent.astype(jnp.bfloat16)


def sum_kernel(keep_ref, came_ref, total_ref, send_ref):
    total = keep_ref[...] + came_ref[...].astype(jnp.float32)
    total_ref[...] = total
    send_ref[...] = total.astype(jnp.bfloat16)


def scale_kernel(start, keep_ref, came_ref, gain_ref, after_ref, out_ref):
    rows, size = keep_ref.shape
    half = gain_ref.shape[1] // 2
    core = lax.rem(lax.axis_index("wide"), 2)
    gain = jnp.where(
        core == 0,
        gain_ref[:, start : start + size],
        gain_ref[:, half + start : half + start + size],
    )
    scaled = gain * (keep_ref[...] + came_ref[...].astype(jnp.float32))
    out_ref[:, :size] = scaled.astype(jnp.bfloat16)
    left = jnp.sum(scaled * scaled, axis=-1, keepdims=True)
    lane = lax.broadcasted_iota(jnp.int32, (rows, LANES), 1)
    tail = jnp.zeros((rows, LANES), jnp.float32)
    for piece in range(3):
        part = left.astype(jnp.bfloat16).astype(jnp.float32)
        tail = jnp.where(lane == piece, part, tail)
        left = left - part
    out_ref[:, size:] = tail.astype(jnp.bfloat16)


def chunk_scores(
    mine, start, near_ref, far_ref, wanted_ref, codes_ref, scales_ref, picks_ref, rows_ref
):
    side_rows, wide = near_ref.shape
    size = wide - LANES
    lists, list_rows, width = codes_ref.shape
    half = width // 2
    pairs = wanted_ref.shape[0]
    row = wanted_ref[:, 0:1]
    local = wanted_ref[:, 1:2]
    column = lax.broadcasted_iota(jnp.int32, (pairs, side_rows), 1)

    def pick(ref, first):
        hot = jnp.where(column + first == row, 1.0, 0.0).astype(jnp.bfloat16)
        return jnp.dot(hot, ref[...], preferred_element_type=jnp.float32)

    chosen = pick(near_ref, 0) + pick(far_ref, side_rows)
    picks_ref[...] = chosen[:, :size].astype(jnp.bfloat16)
    nothing = jnp.zeros((pairs, BLOCK), jnp.bfloat16)
    for block in range(size // BLOCK):
        span = slice(block * BLOCK, (block + 1) * BLOCK)
        kept = block % 2
        rows_ref[kept * pairs : (kept + 1) * pairs, span] = picks_ref[:, span]
        rows_ref[(1 - kept) * pairs : (2 - kept) * pairs, span] = nothing
    squares = jnp.sum(chosen[:, size:], axis=1, keepdims=True)

    core = lax.rem(lax.axis_index("wide"), 2)
    which = core if mine else 1 - core
    blocks = size // BLOCK
    here = pl.ds(
        pl.multiple_of(which * (half // BLOCK) + start // BLOCK, blocks), blocks
    )
    picked = jnp.zeros((pairs, list_rows), jnp.float32)
    for first in range(0, lists, 2):
        scale = jnp.concatenate([scales_ref[first, here, :], scales_ref[first + 1, here, :]], axis=1)
        total = jnp.zeros((pairs, 2 * list_rows), jnp.float32)
        for step in range(blocks // 2):
            span = slice(step * 2 * BLOCK, (step + 1) * 2 * BLOCK)
            away = my_span(mine, half, start + step * 2 * BLOCK, 2 * BLOCK)
            part = lax.dot_general(
                rows_ref[:, span],
                codes_ref[first : first + 2, :, away].reshape(2 * list_rows, 2 * BLOCK),
                (((1,), (1,)), ((), ())),
                preferred_element_type=jnp.float32,
            )
            total += part[:pairs] * scale[2 * step : 2 * step + 1, :]
            total += part[pairs:] * scale[2 * step + 1 : 2 * step + 2, :]
        picked = jnp.where(local == first, total[:, :list_rows], picked)
        picked = jnp.where(local == first + 1, total[:, list_rows:], picked)
    return picked, squares


def some_scores_kernel(
    mine, start, near_ref, far_ref, wanted_ref, codes_ref, scales_ref, *rest
):
    *sofar, picked_ref, squares_ref, picks_ref, rows_ref = rest
    picked, squares = chunk_scores(
        mine, start, near_ref, far_ref, wanted_ref, codes_ref, scales_ref, picks_ref, rows_ref
    )
    if sofar:
        picked += sofar[0][...]
        squares = squares + sofar[1][...]
    picked_ref[...] = picked
    squares_ref[...] = jnp.broadcast_to(squares, squares_ref.shape)


def last_scores_kernel(mine, starts, *refs):
    chunks = len(starts)
    tables = refs[2 * chunks : 2 * chunks + 3]
    sofar_ref, squares_ref, out_ref, picks_ref, rows_ref = refs[2 * chunks + 3 :]
    scores, squares = sofar_ref[...], squares_ref[:, 0:1]
    for c, start in enumerate(starts):
        picked, more = chunk_scores(
            mine, start, refs[2 * c], refs[2 * c + 1], *tables, picks_ref.at[c], rows_ref.at[c]
        )
        scores += picked
        squares = squares + more
    scores = scores * lax.rsqrt(squares + 1e-06)
    devices, capacity, _ = out_ref.shape
    for rank in range(capacity):
        out_ref[:, rank, :] = scores[rank * devices : (rank + 1) * devices]


def sort_merged(a):
    step = len(a) // 2
    while step:
        for i in range(len(a)):
            if i % (2 * step) < step:
                a[i], a[i + step] = jnp.maximum(a[i], a[i + step]), jnp.minimum(a[i], a[i + step])
        step //= 2
    return a


def best_kernel(back_ref, route_ref, out_ref):
    q_dev, count = out_ref.shape
    sources, slots, list_rows = back_ref.shape
    pairs = sources * slots
    scores = back_ref[...].reshape(pairs, list_rows)
    query = route_ref[:, 0:1]
    alive = lax.broadcasted_iota(jnp.int32, (pairs, list_rows), 1) < route_ref[:, 2:3]
    lists = []
    for q in range(q_dev):
        left = jnp.where(alive & (query == q), scores, floor_score)
        tiles = [[left[start : start + SUBLANES]] for start in range(0, pairs, SUBLANES)]
        while len(tiles) > 1:
            merged = [
                sort_merged(one + two[::-1]) for one, two in zip(tiles[::2], tiles[1::2])
            ]
            tiles = [a[:count] for a in merged]
        a = tiles[0]
        shift = SUBLANES // 2
        while shift:
            b = [pltpu.roll(v, shift, 0) for v in a][::-1]
            if 2 * len(a) <= count:
                a = sort_merged(a + b)
            else:
                a = sort_merged([jnp.maximum(one, two) for one, two in zip(a, b)])
            shift //= 2
        lists.append(a)
    place = lax.broadcasted_iota(jnp.int32, (SUBLANES, list_rows), 0)
    a = []
    for rank in range(count):
        v = lists[0][rank]
        for q in range(1, q_dev):
            v = jnp.where(place == q, lists[q][rank], v)
        a.append(v)
    shift = list_rows // 2
    while shift:
        b = [pltpu.roll(v, shift, 1) for v in a][::-1]
        a = sort_merged([jnp.maximum(one, two) for one, two in zip(a, b)])
        shift //= 2
    lane = lax.broadcasted_iota(jnp.int32, (SUBLANES, list_rows), 1)
    out = a[0]
    for rank in range(1, count):
        out = jnp.where(lane == rank, a[rank], out)
    out_ref[...] = out[:q_dev, :count]


def body(
    hidden_in,
    ffn_gain,
    gate_weight,
    up_weight,
    down_weight,
    final_gain,
    codes,
    scales,
    counts,
    list_slot,
    probes,
):
    q_dev, width = hidden_in.shape
    hidden_units = gate_weight.shape[1]
    n = lax.axis_size("wide")
    half = width // 2
    rows = n * q_dev
    lists_dev, list_rows, _ = codes.shape
    capacity = (q_dev * PROBES + n - 1) // n
    mib = 1 << 20
    f32, bf16 = jnp.float32, jnp.bfloat16

    def exchange(x):
        return lax.all_to_all(x, "wide", 0, 0, tiled=True)

    def swapped(x, bit):
        return lax.ppermute(x, "wide", [(i, i ^ bit) for i in range(n)])

    gate_near = pltpu.with_memory_space_constraint(gate_weight, VMEM)
    up_near = pltpu.with_memory_space_constraint(up_weight, VMEM)
    down_near = pltpu.with_memory_space_constraint(down_weight, VMEM)
    codes_near = pltpu.with_memory_space_constraint(codes, VMEM)

    normed = pl.pallas_call(
        norm_kernel,
        out_shape=shaped((q_dev, width + LANES), bf16),
        in_specs=[pl.BlockSpec(memory_space=pltpu.HBM)] * 3,
        out_specs=pl.BlockSpec(memory_space=VMEM),
        scratch_shapes=[
            VMEM((q_dev, width), bf16),
            VMEM((1, width), f32),
            VMEM(probes.shape, jnp.int32),
            pltpu.SemaphoreType.DMA((3,)),
        ],
        compiler_params=pltpu.CompilerParams(vmem_limit_bytes=8 * mib),
    )(
        pltpu.with_memory_space_constraint(hidden_in, pltpu.HBM),
        pltpu.with_memory_space_constraint(ffn_gain[None], pltpu.HBM),
        pltpu.with_memory_space_constraint(probes, pltpu.HBM),
    )
    spread = call(
        spread_kernel,
        shaped((n, q_dev, half + LANES), bf16),
        (normed,),
        8 * mib,
        cost=ahead(gate_weight, up_weight, down_weight),
    )
    here = exchange(spread)
    there = swapped(here, 1)
    gate_part, up_part = call(
        first_kernel,
        [shaped((rows, hidden_units), f32)] * 2,
        (here, gate_near, up_near, down_near),
        8 * mib,
        cost=products(rows * half * hidden_units * 2),
        scratch=[VMEM((rows, half), bf16)],
    )
    size = half // CHUNKS
    starts = [c * size for c in range(CHUNKS)]
    share = shaped((rows + 2 * q_dev, size), bf16)
    act, sent = call(
        second_kernel,
        [shaped((rows, hidden_units), bf16), share],
        (there, gate_part, up_part, gate_near, up_near, down_near, hidden_in),
        8 * mib,
        scratch=[VMEM((rows, half), bf16)],
    )
    work = products(rows * size * hidden_units)
    side_rows = rows // 2
    kept = [shaped((side_rows, size), f32), shaped((side_rows, size), bf16)]
    keep, came = [], []
    for c, start in enumerate(starts):
        if c:
            sent = call(
                functools.partial(share_kernel, half, start),
                share,
                (act, down_near, hidden_in, own),
                8 * mib,
                cost=work,
            )
        crossed = swapped(sent, 1)
        own = call(
            functools.partial(own_kernel, half, start),
            shaped((rows, size), f32),
            (act, down_near),
            8 * mib,
            cost=work,
        )
        total, sent = call(
            functools.partial(side_kernel, start), kept, (own, crossed, hidden_in), 8 * mib
        )
        keep.append(total)
        came.append(swapped(sent, 2))
    bit = 4
    while bit < n:
        for c in range(CHUNKS):
            keep[c], sent = call(
                sum_kernel,
                kept,
                (keep[c], came[c]),
                8 * mib,
                cost=ahead(codes) if bit == 4 and c == 0 else None,
            )
            came[c] = swapped(sent, bit)
        bit *= 2
    route = call(
        functools.partial(route_kernel, lists_dev, capacity),
        shaped((n * capacity, LANES), jnp.int32),
        (probes, list_slot[None], counts[None], keep[-1]),
        4 * mib,
    )
    wanted = call(
        functools.partial(wanted_kernel, capacity, q_dev, PROBES),
        shaped((n * capacity, LANES), jnp.int32),
        (here, list_slot[None], route),
        4 * mib,
    )
    near = [
        call(
            functools.partial(scale_kernel, start),
            shaped((side_rows, size + LANES), bf16),
            (keep[c], came[c], final_gain[None], wanted),
            8 * mib,
        )
        for c, start in enumerate(starts)
    ]
    far = []
    for x in near:
        far.append(swapped(x, 2))
    near_other = []
    for x in near:
        near_other.append(swapped(x, 1))
    far_other = []
    for x in far:
        far_other.append(swapped(x, 1))
    scales_near = jnp.swapaxes(scales, 1, 2)
    pairs = n * capacity
    sofar = []
    for c, start in enumerate(starts):
        sofar = call(
            functools.partial(some_scores_kernel, True, start),
            [shaped((pairs, list_rows), f32), shaped((pairs, LANES), f32)],
            (near[c], far[c], wanted, codes_near, scales_near, *sofar),
            8 * mib,
            cost=products(pairs * lists_dev * list_rows * size),
            scratch=[VMEM((pairs, size), bf16), VMEM((2 * pairs, size), bf16)],
        )
    others = [x for pair in zip(near_other, far_other) for x in pair]
    scores = call(
        functools.partial(last_scores_kernel, False, starts),
        shaped((n, capacity, list_rows), f32),
        (*others, wanted, codes_near, scales_near, *sofar),
        8 * mib,
        scratch=[VMEM((CHUNKS, pairs, size), bf16), VMEM((CHUNKS, 2 * pairs, size), bf16)],
    )
    back = exchange(scores)
    return call(best_kernel, shaped((q_dev, K_TOP), f32), (back, route), 8 * mib)


def solution(mesh):
    in_specs = (
        P(("grp", "wide"), None),
        P(),
        P(None, "wide"),
        P(None, "wide"),
        P("wide", None),
        P(),
        P(("grp", "wide"), None, None),
        P(("grp", "wide"), None, None),
        P("grp"),
        P("grp"),
        P(("grp", "wide"), None),
    )
    out_specs = P(("grp", "wide"), None)
    return jax.shard_map(body, mesh=mesh, in_specs=in_specs, out_specs=out_specs, check_vma=False)
```
